32 devices in a mesh: groups: 2 (over y), tm: 4 (over z), band: 2 (over x), tmpl: 2 (over core).
Axes of the slice: x: 2, y: 2, z: 4, core: 2. Of those that a mesh axis runs over, the one named last changes fastest.
Arguments:
- sft_bins: float32 [2, 128, 2048], P(None, ('groups', 'tm'), 'band'), parts along dimension 1, may hold values from -6 to 6
- delay_code: int32 [8, 128, 1024], P(('groups', 'tmpl'), None, ('tm', 'band')), parts along dimension 0, may hold values from 0 to 16007, as said below
- antenna: float32 [8, 2, 128, 1024], P(('groups', 'tmpl'), None, None, ('tm', 'band')), parts along dimension 0, may hold values from -10 to 10
Outputs:
- f_stat: float32 [8, 128, 8, 128], P(('groups', 'tmpl'), None, ('tm', 'band')), parts along dimension 0
The draws below stay inside these ranges and needn't reach their ends.
There are 2 independent parts, one for each index of `groups`. The reference program is written for one: setup_inputs(seed, part) draws one part's arguments, and reference() takes and returns one part's arrays. A program takes and returns all parts, laid end to end along the dimension named above; each array names one. Nothing has to cross between parts.
Inputs may be any that keep to these rules, and one draw needn't show every extreme that they name: `delay_code`: the whole delay o of a template is the same for all samples n of each aligned run of 256 samples (n // 256 equal).
All inputs are finite; a program needn't handle non-finite values.
Results may differ from the reference program's by a relative error of at most 0.0003.
Values sent between devices are 32-bit elements; how exact they have to be, the bound alone decides.
No kernel may reach another device: no remote copies, remote signals or barrier semaphores. Data moves between devices by JAX's collectives and lax.ppermute only.
A program may use at most 64 MiB of HBM per device.

```python
import math
import jax
import jax.numpy as jnp
from jax import lax

NB = 2048
NQ = 128
NP = 16
SFT_DEV = 8
MAXD = 1000
NFRAC = 8
RUN = 256
NI = 8
NSFT = 64
SAMPLES = 131072
TEMPLATES = 4


def draw_delay_code(key, part):
    blocks = SAMPLES // RUN
    offsets = jax.random.randint(jax.random.fold_in(key, 1), (TEMPLATES, blocks), -MAXD, MAXD + 1)
    block_at = jnp.arange(blocks, dtype=jnp.int32)
    span_len = SFT_DEV * NB
    first_run = (block_at * RUN % span_len == 0)[None, :]
    last_run = ((block_at + 1) * RUN % span_len == 0)[None, :]
    lead_row = (jnp.arange(TEMPLATES, dtype=jnp.int32) == 0)[:, None]
    offsets = jnp.where(first_run & lead_row, -MAXD, offsets)
    offsets = jnp.where(last_run & lead_row, MAXD, offsets)
    offsets = jnp.repeat(offsets, RUN, axis=1)
    fraction = jax.random.randint(jax.random.fold_in(key, 2), (TEMPLATES, SAMPLES), 0, NFRAC)
    fraction = fraction.at[0, 0].set(0)
    fraction = fraction.at[0, SAMPLES - 1].set(NFRAC - 1)
    coded_rows = NFRAC * (offsets + MAXD) + fraction
    coded_rows = coded_rows.reshape(TEMPLATES, NSFT, NQ, NP).transpose(0, 2, 1, 3)
    return coded_rows.reshape(TEMPLATES, NQ, NSFT * NP).astype(jnp.int32)


def draw_antenna(key, part):
    moment = (jnp.arange(SAMPLES, dtype=jnp.float32) + 0.5) / SAMPLES
    lift_ratio = 2.0
    basis_a = jnp.clip(jax.random.normal(jax.random.fold_in(key, 1), (TEMPLATES, SAMPLES), jnp.float32), -4.0, 4.0)
    basis_b = jnp.clip(jax.random.normal(jax.random.fold_in(key, 2), (TEMPLATES, SAMPLES), jnp.float32), -4.0, 4.0)
    ranked = jax.random.permutation(jax.random.fold_in(key, 3), TEMPLATES)
    strong = (ranked < TEMPLATES // 2)[:, None]
    high_coupling = jax.random.uniform(jax.random.fold_in(key, 4), (TEMPLATES, 1), jnp.float32, 0.95, 0.99)
    low_coupling = jax.random.uniform(jax.random.fold_in(key, 5), (TEMPLATES, 1), jnp.float32, -0.4, 0.4)
    coupling = jnp.where(strong, high_coupling, low_coupling)
    envelope_a = jnp.sqrt(1.0 + lift_ratio * moment)
    envelope_b = jnp.sqrt(1.0 + lift_ratio * (1.0 - moment))
    weight_a = envelope_a * basis_a
    weight_b = envelope_b * (coupling * basis_a + jnp.sqrt(1.0 - coupling * coupling) * basis_b)
    stacked = jnp.stack([weight_a, weight_b], axis=1)
    stacked = stacked.reshape(TEMPLATES, 2, NSFT, NQ, NP).transpose(0, 1, 3, 2, 4)
    return stacked.reshape(TEMPLATES, 2, NQ, NSFT * NP).astype(jnp.float32)


def shard_levels(own_key, shape, pieces, smallest, top_value):
    def one(position, parts):
        draws = jax.random.uniform(jax.random.fold_in(jax.random.fold_in(own_key, 6), position), (parts,), jnp.float32, smallest / len(pieces), top_value / len(pieces))
        return jnp.repeat(jnp.exp(draws), shape[position] // parts).reshape((-1,) + (1,) * (len(shape) - position - 1))

    gain = one(*pieces[0])
    for cut in pieces[1:]:
        gain = gain * one(*cut)
    return gain


def gaussian(own_key, extent, width, bound, shards=(), kind=jnp.bfloat16):
    entries = width * jax.random.normal(own_key, extent, jnp.float32)
    if shards:
        entries = entries * shard_levels(own_key, extent, shards, -0.22, 0.18)
    return jnp.clip(entries, -bound, bound).astype(kind)


def setup_inputs(seed: int = 0, part: int = 0) -> dict:
    arg_keys = jax.random.split(jax.random.key(seed), 4)
    part_keys = jax.random.split(jax.random.fold_in(arg_keys[3], part), 4)
    return {
        "sft_bins": gaussian(part_keys[0], (2, NSFT, NB), 1.0, 6.0, ((1, 4), (2, 2)), jnp.float32),
        "delay_code": draw_delay_code(jax.random.fold_in(jax.random.fold_in(arg_keys[3], part), 71), part),
        "antenna": draw_antenna(jax.random.fold_in(jax.random.fold_in(arg_keys[3], part), 71), part),
    }


stat_eps = 1e-06
floor_share = 0.5

def lagrange(fraction):
    return (-fraction * (fraction - 1.0) * (fraction - 2.0) / 6.0, (fraction + 1.0) * (fraction - 1.0) * (fraction - 2.0) / 2.0, -(fraction + 1.0) * fraction * (fraction - 2.0) / 2.0, (fraction + 1.0) * fraction * (fraction - 1.0) / 6.0)

def reference(sft_bins, delay_code, antenna):
    spectrum = lax.complex(sft_bins[0], sft_bins[1])
    series = (jnp.fft.ifft(spectrum, axis=1) * math.sqrt(NB)).reshape(SAMPLES)
    margin = MAXD + 2
    padding = jnp.zeros((margin,), series.dtype)
    padded = jnp.concatenate([padding, series, padding])
    code_rows = delay_code.reshape(TEMPLATES, NQ, NSFT, NP).transpose(0, 2, 1, 3).reshape(TEMPLATES, SAMPLES)
    weight_rows = antenna.reshape(TEMPLATES, 2, NQ, NSFT, NP).transpose(0, 1, 3, 2, 4).reshape(TEMPLATES, 2, SAMPLES)

    def one_template(inputs):
        code_row, weights = inputs
        offsets = code_row // NFRAC - MAXD
        fraction = (code_row % NFRAC).astype(jnp.float32) / NFRAC
        coeffs = lagrange(fraction)
        base_pos = jnp.arange(SAMPLES, dtype=jnp.int32) + offsets - 1 + margin
        resampled = coeffs[0] * padded[base_pos]
        for tap_index in range(1, 4):
            resampled = resampled + coeffs[tap_index] * padded[base_pos + tap_index]
        weight_a = weights[0]
        weight_b = weights[1]
        spec_a = jnp.fft.fft(weight_a * resampled) / math.sqrt(SAMPLES)
        spec_b = jnp.fft.fft(weight_b * resampled) / math.sqrt(SAMPLES)
        power_a = jnp.mean(weight_a * weight_a) + stat_eps
        power_b = jnp.mean(weight_b * weight_b) + stat_eps
        cross_ab = jnp.mean(weight_a * weight_b)
        det_floor = jnp.maximum(power_a * power_b - cross_ab * cross_ab, floor_share * power_a * power_b)
        a_real, a_imag = (jnp.real(spec_a), jnp.imag(spec_a))
        b_real, b_imag = (jnp.real(spec_b), jnp.imag(spec_b))
        f_stat = (power_b * (a_real * a_real + a_imag * a_imag) + power_a * (b_real * b_real + b_imag * b_imag) - 2.0 * cross_ab * (a_real * b_real + a_imag * b_imag)) / det_floor
        return f_stat.reshape(NP, NQ, SFT_DEV, NI).transpose(1, 3, 2, 0).reshape(NQ, NI, SFT_DEV * NP)
    return lax.map(one_template, (code_rows, weight_rows))
```

```python
import functools
import math

import jax
import jax.numpy as jnp
import numpy as np
from jax import lax
from jax.experimental import pallas as pl
from jax.experimental.pallas import tpu as pltpu
from jax.sharding import PartitionSpec as P

NB = 2048
NQ = 128
NP = 16
SFT_DEV = 8
MAXD = 1000
NFRAC = 8
RUN = 256


stat_eps = 1e-06
floor_share = 0.5


def shifted(value, axis, by):
    length = lax.axis_size(axis)
    pairs = [(i, i + by) for i in range(length) if 0 <= i + by < length]
    return lax.ppermute(value, axis, pairs)


def lagrange(fraction):
    return (
        -fraction * (fraction - 1.0) * (fraction - 2.0) / 6.0,
        (fraction + 1.0) * (fraction - 1.0) * (fraction - 2.0) / 2.0,
        -(fraction + 1.0) * fraction * (fraction - 2.0) / 2.0,
        (fraction + 1.0) * fraction * (fraction - 1.0) / 6.0,
    )


def phase_pair(product, modulus, direction):
    angles = direction * 2.0 * math.pi / modulus * (product % modulus).astype(jnp.float32)
    return (jnp.cos(angles), jnp.sin(angles))


def dft_table(length, direction):
    rows_at = lax.broadcasted_iota(jnp.int32, (length, length), 0)
    cols_at = lax.broadcasted_iota(jnp.int32, (length, length), 1)
    return phase_pair(rows_at * cols_at, length, direction)


def complex_einsum(pattern, lhs_pair, rhs_pair):
    lhs_real, lhs_imag = lhs_pair
    rhs_real, rhs_imag = rhs_pair
    high = lax.Precision.HIGHEST
    out_real = jnp.einsum(pattern, lhs_real, rhs_real, precision=high) - jnp.einsum(
        pattern, lhs_imag, rhs_imag, precision=high
    )
    out_imag = jnp.einsum(pattern, lhs_real, rhs_imag, precision=high) + jnp.einsum(
        pattern, lhs_imag, rhs_real, precision=high
    )
    return (out_real, out_imag)


def rotate(values, phases):
    val_real, val_imag = values
    cos_part, sin_part = phases
    return (val_real * cos_part - val_imag * sin_part, val_real * sin_part + val_imag * cos_part)


def apply_weights(arrived):
    return arrived[:, 1][:, :, None] * arrived[:, 0][:, None]


def finish(arrived):
    owners = lax.axis_size("tm") * lax.axis_size("band")
    my_rank = lax.axis_index("tm") * lax.axis_size("band") + lax.axis_index("band")
    q_local = arrived.shape[3]
    lane_width = arrived.shape[5]
    sample_total = SFT_DEV * owners * NB
    section_one = complex_einsum(
        "abqix,ic->abqcx", (arrived[:, :, 0], arrived[:, :, 1]), dft_table(owners, -1.0)
    )
    c_pos = lax.broadcasted_iota(jnp.int32, (owners, lane_width), 0)
    x_pos = lax.broadcasted_iota(jnp.int32, (owners, lane_width), 1)
    section_one = rotate(section_one, phase_pair(c_pos * (x_pos // NP), SFT_DEV * owners, -1.0))
    short_table = dft_table(SFT_DEV, -1.0)
    ident_rows = jnp.eye(NP, dtype=jnp.float32)
    spread = (jnp.kron(short_table[0], ident_rows), jnp.kron(short_table[1], ident_rows))
    section_two = complex_einsum("abqcx,xy->abqcy", section_one, spread)
    q_grid = my_rank * q_local + lax.broadcasted_iota(jnp.int32, (q_local, owners, lane_width), 0)
    c_grid = lax.broadcasted_iota(jnp.int32, (q_local, owners, lane_width), 1)
    x_grid = lax.broadcasted_iota(jnp.int32, (q_local, owners, lane_width), 2)
    time_index = x_grid % NP + NP * q_grid
    freq_index = c_grid + owners * (x_grid // NP)
    section_two = rotate(section_two, phase_pair(time_index * freq_index, sample_total, -1.0))
    packed = jnp.stack(section_two, axis=2)
    turned = lax.all_to_all(packed, ("tm", "band"), split_axis=4, concat_axis=3, tiled=True)
    turned = turned.reshape(turned.shape[0], 2, 2, NQ, lane_width)
    section_three = complex_einsum(
        "abqx,qv->abvx", (turned[:, :, 0], turned[:, :, 1]), dft_table(NQ, -1.0)
    )
    v_pos = lax.broadcasted_iota(jnp.int32, (NQ, lane_width), 0)
    p_pos = lax.broadcasted_iota(jnp.int32, (NQ, lane_width), 1) % NP
    section_three = rotate(section_three, phase_pair(v_pos * p_pos, NB, -1.0))
    fine_table = dft_table(NP, -1.0)
    ident_blocks = jnp.eye(SFT_DEV, dtype=jnp.float32)
    block_table = (jnp.kron(ident_blocks, fine_table[0]), jnp.kron(ident_blocks, fine_table[1]))
    result = complex_einsum("abvx,xy->abvy", section_three, block_table)
    return jnp.stack(result, axis=2)


def per_device(sft_bins, delay_code, antenna):
    owners = lax.axis_size("tm") * lax.axis_size("band")
    sample_total = SFT_DEV * owners * NB
    spectra = lax.all_to_all(sft_bins, "band", split_axis=1, concat_axis=2, tiled=True)
    bin_grid = spectra.reshape(2, SFT_DEV, NP, NQ)
    section_one = complex_einsum("pk,skl->spl", dft_table(NP, 1.0), (bin_grid[0], bin_grid[1]))
    p_rows = lax.broadcasted_iota(jnp.int32, (NP, NQ), 0)
    l_cols = lax.broadcasted_iota(jnp.int32, (NP, NQ), 1)
    section_one = rotate(section_one, phase_pair(p_rows * l_cols, NB, 1.0))
    series_pair = complex_einsum("spl,lq->spq", section_one, dft_table(NQ, 1.0))
    norm_scale = 1.0 / math.sqrt(NB)
    stacked = jnp.stack([series_pair[0] * norm_scale, series_pair[1] * norm_scale])
    rim_cols = (MAXD + 1 + NP) // NP
    head_rim = stacked[:, 0, :, :rim_cols]
    tail_rim = stacked[:, SFT_DEV - 1, :, NQ - rim_cols :]
    after_rim = shifted(head_rim, ("tm", "band"), -1)
    before = shifted(tail_rim, ("tm", "band"), 1)
    rim_size = NP * rim_cols
    span_len = SFT_DEV * NB
    timed = stacked.transpose(0, 1, 3, 2).reshape(2, span_len)
    before_timed = before.transpose(0, 2, 1).reshape(2, rim_size)
    after_timed = after_rim.transpose(0, 2, 1).reshape(2, rim_size)
    buffer = jnp.concatenate([before_timed, timed, after_timed], axis=1)
    lane_width = SFT_DEV * NP
    tmpl_local = delay_code.shape[0]
    run_count = span_len // RUN
    code_time = (
        delay_code.reshape(tmpl_local, NQ, SFT_DEV, NP)
        .transpose(0, 2, 1, 3)
        .reshape(tmpl_local, run_count, RUN)
    )
    offsets = code_time[:, :, 0] // NFRAC - MAXD
    run_starts = (jnp.arange(run_count, dtype=jnp.int32) * RUN)[None, :] + offsets + (rim_size - 1)

    def take_segment(start):
        return lax.dynamic_slice_in_dim(buffer, start, RUN + 3, 1)

    segments = jax.vmap(jax.vmap(take_segment))(run_starts)
    fraction = (code_time % NFRAC).astype(jnp.float32) / NFRAC
    coeffs = lagrange(fraction)
    res_time = coeffs[0][:, :, None, :] * segments[:, :, :, 0:RUN]
    for tap_index in range(1, 4):
        res_time = (
            res_time
            + coeffs[tap_index][:, :, None, :] * segments[:, :, :, tap_index : tap_index + RUN]
        )
    resampled = res_time.transpose(0, 2, 1, 3).reshape(tmpl_local, 2, SFT_DEV, NQ, NP)
    resampled = resampled.transpose(0, 1, 3, 2, 4).reshape(tmpl_local, 2, NQ, lane_width)
    weight_a = antenna[:, 0]
    weight_b = antenna[:, 1]
    local_sums = jnp.stack(
        [
            jnp.sum(weight_a * weight_a, axis=(1, 2)),
            jnp.sum(weight_b * weight_b, axis=(1, 2)),
            jnp.sum(weight_a * weight_b, axis=(1, 2)),
        ],
        axis=1,
    )
    totals = lax.psum(local_sums, ("tm", "band"))
    payload = jnp.stack([resampled, antenna], axis=1)
    spectra_out = finish(
        apply_weights(
            lax.all_to_all(
                payload[:, :, :, :, None, :],
                ("tm", "band"),
                split_axis=3,
                concat_axis=4,
                tiled=True,
            )
        )
    )
    out_scale = 1.0 / math.sqrt(sample_total)
    a_real = spectra_out[:, 0, 0] * out_scale
    a_imag = spectra_out[:, 0, 1] * out_scale
    b_real = spectra_out[:, 1, 0] * out_scale
    b_imag = spectra_out[:, 1, 1] * out_scale
    power_a = (totals[:, 0] / sample_total + stat_eps)[:, None, None]
    power_b = (totals[:, 1] / sample_total + stat_eps)[:, None, None]
    cross_ab = (totals[:, 2] / sample_total)[:, None, None]
    det_floor = jnp.maximum(
        power_a * power_b - cross_ab * cross_ab, floor_share * power_a * power_b
    )
    f_stat = (
        power_b * (a_real * a_real + a_imag * a_imag)
        + power_a * (b_real * b_real + b_imag * b_imag)
        - 2.0 * cross_ab * (a_real * b_real + a_imag * b_imag)
    ) / det_floor
    return f_stat[:, :, None, :]


LANES = 128
ROWS = 8
HALO = 2


def split_table(table):
    high = table.astype(jnp.bfloat16)
    low = (table - high.astype(np.float64)).astype(jnp.bfloat16)
    return np.stack([high, low])


def unit(product, modulus, sign):
    angle = sign * 2.0 * np.pi / modulus * (product % modulus)
    return np.cos(angle), np.sin(angle)


def inverse_tables():
    p_at = np.arange(NP)[:, None]
    l_at = np.arange(NQ)[None, :]
    twist = np.stack(unit(p_at * l_at, NB, 1.0)) / math.sqrt(NB)
    real, imag = unit(np.arange(NQ)[:, None] * l_at, NQ, 1.0)
    full = np.block([[real, -imag], [imag, real]])
    return twist.astype(np.float32), split_table(full)


def forward_table():
    lane = np.arange(LANES)
    bins = ROWS * (lane % NP) + lane // NP
    real, imag = unit(np.arange(LANES)[:, None] * bins[None, :], LANES, -1.0)
    return split_table(np.block([[real, imag], [-imag, real]]))


def add(one, two):
    return one[0] + two[0], one[1] + two[1]


def sub(one, two):
    return one[0] - two[0], one[1] - two[1]


def turn(value, step, length, sign):
    real, imag = value
    step = step % length
    if step == 0:
        return value
    if 2 * step == length:
        return -real, -imag
    if 4 * step == length:
        return (-imag, real) if sign > 0 else (imag, -real)
    if 4 * step == 3 * length:
        return (imag, -real) if sign > 0 else (-imag, real)
    angle = sign * 2.0 * math.pi * step / length
    cos_part, sin_part = math.cos(angle), math.sin(angle)
    if 8 * step == length:
        root = math.sqrt(0.5)
        if sign > 0:
            return (real - imag) * root, (real + imag) * root
        return (real + imag) * root, (imag - real) * root
    return real * cos_part - imag * sin_part, real * sin_part + imag * cos_part


def small_fft(values, sign):
    length = len(values)
    if length == 1:
        return values
    if length == 2:
        return [add(values[0], values[1]), sub(values[0], values[1])]
    even = small_fft(values[0::2], sign)
    odd = small_fft(values[1::2], sign)
    half = length // 2
    turned = [turn(odd[k], k, length, sign) for k in range(half)]
    return [add(even[k], turned[k]) for k in range(half)] + [sub(even[k], turned[k]) for k in range(half)]


def times(value, cos_part, sin_part):
    real, imag = value
    return real * cos_part - imag * sin_part, real * sin_part + imag * cos_part


def block_transpose(tile):
    row = lax.broadcasted_iota(jnp.int32, (ROWS, LANES), 0)
    group = lax.broadcasted_iota(jnp.int32, (ROWS, LANES), 1) // NP
    for bit in (1, 2, 4):
        row_bit = (row & bit) != 0
        group_bit = (group & bit) != 0
        up = pltpu.roll(pltpu.roll(tile, ROWS - bit, 0), NP * bit, 1)
        if bit == 4:
            moved = up
        else:
            down = pltpu.roll(pltpu.roll(tile, bit, 0), LANES - NP * bit, 1)
            moved = jnp.where(group_bit, up, down)
        tile = jnp.where(row_bit == group_bit, tile, moved)
    return tile


def split_dot(lhs, rhs, dims):
    out = None
    for one, two in ((0, 0), (0, 1), (1, 0)):
        part = lax.dot_general(lhs[one], rhs[two], dims, preferred_element_type=jnp.float32)
        out = part if out is None else out + part
    return out


def split_value(value):
    high = value.astype(jnp.bfloat16)
    return high, (value - high.astype(jnp.float32)).astype(jnp.bfloat16)


def prepare_kernel(code_ref, antenna_ref, fraction_ref, weights_ref):
    tmpl_local = code_ref.shape[0]
    owners = weights_ref.shape[0]
    stride = weights_ref.shape[1]
    for t in range(tmpl_local):
        for h in range(2):
            for j in range(owners):
                rows = pl.ds(2 * ROWS * j + ROWS * h, ROWS)
                level = (code_ref[t, rows, :] & (NFRAC - 1)).astype(jnp.float32) * (1.0 / NFRAC)
                fraction_ref[pl.ds(t * 128 + h * ROWS + j, ROWS, stride=2 * ROWS), :] = block_transpose(level)
        sums = [jnp.zeros((ROWS, LANES), jnp.float32) for _ in range(3)]
        for h in range(2):
            for j in range(owners):
                rows = pl.ds(2 * ROWS * j + ROWS * h, ROWS)
                one = antenna_ref[t, 0, rows, :]
                two = antenna_ref[t, 1, rows, :]
                sums = [sums[0] + one * one, sums[1] + two * two, sums[2] + one * two]
                for w, tile in ((0, one), (1, two)):
                    weights_ref[j, pl.ds(t * 4 + w * 2 + h, ROWS, stride=ROWS), :] = block_transpose(tile)
        for index in range(3):
            row = jnp.sum(sums[index], axis=0, keepdims=True)
            for j in range(owners):
                weights_ref[j, pl.ds(stride - ROWS + t * 4 + index, 1), :] = row
        for j in range(owners):
            weights_ref[j, pl.ds(stride - ROWS + t * 4 + 3, 1), :] = jnp.zeros((1, LANES), jnp.float32)


def resample_kernel(start_ref, bins_ref, fraction_ref, twist_ref, table_ref, out_ref, z_ref, grid_ref, time_ref, run_ref):
    for g in range(2):
        values = []
        for kappa in range(NP):
            rows, cols = pl.ds(ROWS * g, ROWS), pl.ds(LANES * kappa, LANES)
            values.append((bins_ref[0, rows, cols], bins_ref[1, rows, cols]))
        values = small_fft(values, 1.0)
        for p in range(NP):
            cos_part = twist_ref[0, pl.ds(p, 1), :]
            sin_part = twist_ref[1, pl.ds(p, 1), :]
            turned = times(values[p], cos_part, sin_part)
            for part in range(2):
                z_ref[part, pl.ds(LANES * g + p, ROWS, stride=NP), :] = turned[part]
    dims = (((1,), (1,)), ((), ()))
    grid_ref[...] = split_dot((table_ref[0], table_ref[1]), split_value(jnp.concatenate([z_ref[0], z_ref[1]], axis=1)), dims)
    lane = lax.broadcasted_iota(jnp.int32, (ROWS, LANES), 1)
    per_sft = NB // LANES
    for part in range(2):
        for r in range(per_sft):
            tile = grid_ref[pl.ds(NQ * part + ROWS * r, ROWS), pl.ds(0, LANES)]
            time_ref[pl.ds(2 * (per_sft + r) + part, ROWS, stride=2 * per_sft), :] = block_transpose(tile)
        for r in range(per_sft // 2):
            late = grid_ref[pl.ds(NQ * part + ROWS * (r + per_sft // 2), ROWS), pl.ds(LANES, LANES)]
            early = grid_ref[pl.ds(NQ * part + ROWS * r, ROWS), pl.ds(LANES, LANES)]
            tile = block_transpose(jnp.where(lane < NP, late, early))
            time_ref[pl.ds(2 * (r + per_sft // 2) + part, 1), :] = tile[0:1]
            time_ref[pl.ds(2 * (per_sft * (SFT_DEV + 1) + r) + part, 1), :] = tile[1:2]

    def one_sft(at, carry):
        for j in range(ROWS):
            start = start_ref[at * ROWS + j]
            shift = start & (LANES - 1)
            tile = time_ref[pl.ds((start >> 7) * 2, ROWS), :]
            tile = pltpu.roll(tile, (LANES - shift) & (LANES - 1), 1)
            run_ref[pl.ds(ROWS * j, ROWS), :] = jnp.where(lane < LANES - shift, tile, pltpu.roll(tile, ROWS - 2, 0))
        t, s_local = at >> 3, at & 7
        coeffs = [lagrange(fraction_ref[pl.ds((at * 2 + h) * ROWS, ROWS), :]) for h in range(2)]
        for part in range(2):
            rows = [run_ref[pl.ds(2 * i + part, ROWS, stride=ROWS), :] for i in range(3)]
            totals = [coeffs[h][0] * rows[h] for h in range(2)]
            for k in range(1, 4):
                rolled = [pltpu.roll(row, LANES - k, 1) for row in rows]
                for h in range(2):
                    tap = jnp.where(lane < LANES - k, rolled[h], rolled[h + 1])
                    totals[h] = totals[h] + coeffs[h][k] * tap
            for h in range(2):
                out_ref[pl.ds(s_local * ROWS + t * 4 + part * 2 + h, ROWS, stride=8 * ROWS), :] = totals[h]
        return carry

    lax.fori_loop(0, start_ref.shape[0] // ROWS, one_sft, 0)


def section_kernel(samples_ref, weights_ref, out_ref, sums_ref, mid_ref):
    owners = samples_ref.shape[0]
    row = lax.broadcasted_iota(jnp.int32, (ROWS, LANES), 0)
    imag_row = (row & 2) != 0
    for s_local in range(SFT_DEV):
        values = []
        for i in range(owners):
            pair = samples_ref[i, pl.ds(ROWS * s_local, ROWS), :]
            weight = weights_ref[i, pl.ds(ROWS * s_local, ROWS), :]
            real = jnp.where(imag_row, pltpu.roll(pair, 2, 0), pair)
            imag = jnp.where(imag_row, pair, pltpu.roll(pair, ROWS - 2, 0))
            values.append((real * weight, imag * weight))
        values = small_fft(values, -1.0)
        for c in range(owners):
            turned = turn(values[c], c * s_local, owners * SFT_DEV, -1.0)
            for part in range(2):
                mid_ref[part, pl.ds((c * SFT_DEV + s_local) * ROWS, ROWS), :] = turned[part]
    for c in range(owners):
        values = []
        for s_local in range(SFT_DEV):
            rows = pl.ds((c * SFT_DEV + s_local) * ROWS, ROWS)
            values.append((mid_ref[0, rows, :], mid_ref[1, rows, :]))
        values = small_fft(values, -1.0)
        for d in range(SFT_DEV):
            for part in range(2):
                out_ref[c, pl.ds(part * ROWS * ROWS + d, ROWS, stride=ROWS), :] = values[d][part]
    total = weights_ref[0, pl.ds(SFT_DEV * ROWS, ROWS), :]
    for i in range(1, owners):
        total = total + weights_ref[i, pl.ds(SFT_DEV * ROWS, ROWS), :]
    sums_ref[...] = jnp.broadcast_to(jnp.sum(total, axis=1, keepdims=True), (ROWS, LANES))


def statistic_kernel(sample_total, parts_ref, sums_ref, coarse_ref, fine_ref, table_ref, out_ref):
    rhs = (table_ref[0], table_ref[1])
    dims = (((1,), (0,)), ((), ()))
    tmpl_local = out_ref.shape[0]
    owners = parts_ref.shape[0]
    for t in range(tmpl_local):
        spectra = []
        for w in range(2):
            values = []
            for rho in range(2 * owners):
                j, h = rho // 2, rho % 2
                base = (t * 4 + w * 2 + h) * ROWS
                value = tuple(parts_ref[j, pl.ds(part * ROWS * ROWS + base, ROWS), :] for part in range(2))
                rows = pl.ds(rho * ROWS, ROWS)
                values.append(times(value, coarse_ref[0, rows, :], coarse_ref[1, rows, :]))
            values = small_fft(values, -1.0)
            values = [
                times(values[a], fine_ref[0, pl.ds(a * ROWS, ROWS), :], fine_ref[1, pl.ds(a * ROWS, ROWS), :])
                for a in range(2 * owners)
            ]
            real = jnp.concatenate([value[0] for value in values], axis=0)
            imag = jnp.concatenate([value[1] for value in values], axis=0)
            lhs = split_value(jnp.concatenate([real, imag], axis=1))
            out = split_dot(lhs, rhs, dims)
            spectra.append((out[:, :LANES], out[:, LANES:]))
        (a_real, a_imag), (b_real, b_imag) = spectra
        power_a = sums_ref[pl.ds(t * 4, 1), :] * (1.0 / sample_total) + stat_eps
        power_b = sums_ref[pl.ds(t * 4 + 1, 1), :] * (1.0 / sample_total) + stat_eps
        cross_ab = sums_ref[pl.ds(t * 4 + 2, 1), :] * (1.0 / sample_total)
        det_floor = jnp.maximum(power_a * power_b - cross_ab * cross_ab, floor_share * power_a * power_b)
        f_stat = (
            (power_b / det_floor) * (a_real * a_real + a_imag * a_imag)
            + (power_a / det_floor) * (b_real * b_real + b_imag * b_imag)
            - (2.0 * cross_ab / det_floor) * (a_real * b_real + a_imag * b_imag)
        )
        for a in range(2 * owners):
            tile = block_transpose(f_stat[a * ROWS : (a + 1) * ROWS])
            out_ref[t, pl.ds(a, ROWS, stride=2 * owners), :] = tile


def vmem():
    return pl.BlockSpec(memory_space=pltpu.VMEM)


def exchange_bins(sft_bins):
    owner_count = lax.axis_size("tm") * lax.axis_size("band")
    first = lax.axis_index("band") == 0
    near = jnp.where(
        first,
        jnp.concatenate([sft_bins[:, SFT_DEV:], sft_bins[:, SFT_DEV - 1 : SFT_DEV]], axis=1),
        sft_bins[:, : SFT_DEV + 1],
    )
    tail, head = sft_bins[:, -1:], sft_bins[:, :1]
    same = jnp.where(first, tail, head)
    other = jnp.where(first, head, tail)
    axes = ("tm", "band")
    straight, crossed = [], []
    for rank in range(owner_count):
        up = rank % 2 == 0
        target = rank + 2 if up else rank - 2
        if 0 <= target < owner_count:
            straight.append((rank, target))
        target = rank - 1 if up else rank + 1
        if 0 <= target < owner_count:
            crossed.append((rank, target))
    near = lax.ppermute(near, "band", [(0, 1), (1, 0)])
    same = lax.ppermute(same, axes, straight)
    other = lax.ppermute(other, axes, crossed)
    mine = jnp.where(first, sft_bins[:, :SFT_DEV], sft_bins[:, SFT_DEV:])
    inner = jnp.where(first, sft_bins[:, SFT_DEV : SFT_DEV + 1], sft_bins[:, SFT_DEV - 1 : SFT_DEV])
    my_halo = jnp.where(first, jnp.concatenate([same, inner], axis=1), jnp.concatenate([inner, same], axis=1))
    far_inner = near[:, SFT_DEV:]
    far_halo = jnp.where(
        first, jnp.concatenate([other, far_inner], axis=1), jnp.concatenate([far_inner, other], axis=1)
    )
    blank = jnp.zeros((2, ROWS - HALO, sft_bins.shape[2]), jnp.float32)
    my_rows = jnp.concatenate([mine, my_halo, blank], axis=1)
    far_rows = jnp.concatenate([near[:, :SFT_DEV], far_halo, blank], axis=1)
    return jnp.concatenate(
        [jnp.where(first, my_rows, far_rows), jnp.where(first, far_rows, my_rows)], axis=2
    )


def run_device(sft_bins, delay_code, antenna):
    axes = ("tm", "band")
    owners = lax.axis_size("tm") * lax.axis_size("band")
    my_rank = lax.axis_index("tm") * lax.axis_size("band") + lax.axis_index("band")
    sample_total = SFT_DEV * owners * NB
    tmpl_local = delay_code.shape[0]
    run_count = SFT_DEV * NB // RUN
    f32 = jnp.float32
    bins = exchange_bins(sft_bins)
    slot = SFT_DEV * ROWS
    fraction, weights = pl.pallas_call(
        prepare_kernel,
        out_shape=(
            jax.ShapeDtypeStruct((tmpl_local * SFT_DEV * 2 * ROWS, LANES), f32),
            jax.ShapeDtypeStruct((owners, slot + ROWS, LANES), f32),
        ),
        in_specs=[vmem(), vmem()],
        out_specs=(vmem(), vmem()),
        name="prepare",
    )(delay_code, antenna)
    weights = lax.all_to_all(weights, axes, split_axis=0, concat_axis=0, tiled=True)
    offsets = delay_code[:, :: RUN // NP, ::NP] // NFRAC - MAXD
    offsets = offsets.transpose(0, 2, 1).reshape(tmpl_local, run_count)
    starts = (jnp.arange(run_count, dtype=jnp.int32) * RUN)[None, :] + offsets + (NB - 1)
    twist, inverse_table = inverse_tables()
    samples = pl.pallas_call(
        resample_kernel,
        out_shape=jax.ShapeDtypeStruct((owners * slot, LANES), f32),
        in_specs=[pl.BlockSpec(memory_space=pltpu.SMEM)] + [vmem()] * 4,
        out_specs=vmem(),
        scratch_shapes=[
            pltpu.VMEM((2, 2 * LANES, LANES), f32),
            pltpu.VMEM((2 * LANES, 2 * LANES), f32),
            pltpu.VMEM((2 * (SFT_DEV + 2) * NB // LANES, LANES), f32),
            pltpu.VMEM((ROWS * ROWS, LANES), f32),
        ],
        name="resample",
    )(starts.reshape(-1), bins, fraction, jnp.asarray(twist), jnp.asarray(inverse_table))
    samples = lax.all_to_all(samples.reshape(owners, slot, LANES), axes, split_axis=0, concat_axis=0, tiled=True)
    parts, sums = pl.pallas_call(
        section_kernel,
        out_shape=(
            jax.ShapeDtypeStruct((owners, 2 * slot, LANES), f32),
            jax.ShapeDtypeStruct((ROWS, LANES), f32),
        ),
        in_specs=[vmem(), vmem()],
        out_specs=(vmem(), vmem()),
        scratch_shapes=[pltpu.VMEM((2, owners * slot, LANES), f32)],
        name="section",
    )(samples, weights)
    parts = lax.all_to_all(parts, axes, split_axis=0, concat_axis=0, tiled=True)
    row = lax.broadcasted_iota(jnp.int32, (2 * owners * ROWS, LANES), 0)
    lane = lax.broadcasted_iota(jnp.int32, (2 * owners * ROWS, LANES), 1)
    freq = my_rank + owners * (row % ROWS)
    coarse = jnp.stack(phase_pair((row // ROWS) * freq, sample_total // LANES, -1.0))
    fine = jnp.stack(phase_pair(lane * (freq + owners * SFT_DEV * (row // ROWS)), sample_total, -1.0))
    fine = fine * (1.0 / math.sqrt(sample_total))
    f_stat = pl.pallas_call(
        functools.partial(statistic_kernel, sample_total),
        out_shape=jax.ShapeDtypeStruct((tmpl_local, NQ, LANES), f32),
        in_specs=[vmem()] * 5,
        out_specs=vmem(),
        name="statistic",
    )(parts, sums, coarse, fine, jnp.asarray(forward_table()))
    return f_stat[:, :, None, :]


def solution(mesh):
    owners = mesh.shape["tm"] * mesh.shape["band"]
    one_run_each = NB // RUN == owners and mesh.shape["band"] == 2
    in_specs = (
        P(None, ("groups", "tm"), "band"),
        P(("groups", "tmpl"), None, ("tm", "band")),
        P(("groups", "tmpl"), None, None, ("tm", "band")),
    )
    out_specs = P(("groups", "tmpl"), None, ("tm", "band"), None)
    return jax.shard_map(
        run_device if one_run_each else per_device,
        mesh=mesh,
        in_specs=in_specs,
        out_specs=out_specs,
        check_vma=False,
    )
```

```python
import functools
import math

import jax
import jax.numpy as jnp
import numpy as np
from jax import lax
from jax.experimental import pallas as pl
from jax.experimental.pallas import tpu as pltpu
from jax.sharding import PartitionSpec as P

NB = 2048
NQ = 128
NP = 16
SFT_DEV = 8
MAXD = 1000
NFRAC = 8
RUN = 256


stat_eps = 1e-06
floor_share = 0.5


def shifted(value, axis, by):
    length = lax.axis_size(axis)
    pairs = [(i, i + by) for i in range(length) if 0 <= i + by < length]
    return lax.ppermute(value, axis, pairs)


def lagrange(fraction):
    return (
        -fraction * (fraction - 1.0) * (fraction - 2.0) / 6.0,
        (fraction + 1.0) * (fraction - 1.0) * (fraction - 2.0) / 2.0,
        -(fraction + 1.0) * fraction * (fraction - 2.0) / 2.0,
        (fraction + 1.0) * fraction * (fraction - 1.0) / 6.0,
    )


def phase_pair(product, modulus, direction):
    angles = direction * 2.0 * math.pi / modulus * (product % modulus).astype(jnp.float32)
    return (jnp.cos(angles), jnp.sin(angles))


def dft_table(length, direction):
    rows_at = lax.broadcasted_iota(jnp.int32, (length, length), 0)
    cols_at = lax.broadcasted_iota(jnp.int32, (length, length), 1)
    return phase_pair(rows_at * cols_at, length, direction)


def complex_einsum(pattern, lhs_pair, rhs_pair):
    lhs_real, lhs_imag = lhs_pair
    rhs_real, rhs_imag = rhs_pair
    high = lax.Precision.HIGHEST
    out_real = jnp.einsum(pattern, lhs_real, rhs_real, precision=high) - jnp.einsum(
        pattern, lhs_imag, rhs_imag, precision=high
    )
    out_imag = jnp.einsum(pattern, lhs_real, rhs_imag, precision=high) + jnp.einsum(
        pattern, lhs_imag, rhs_real, precision=high
    )
    return (out_real, out_imag)


def rotate(values, phases):
    val_real, val_imag = values
    cos_part, sin_part = phases
    return (val_real * cos_part - val_imag * sin_part, val_real * sin_part + val_imag * cos_part)


def apply_weights(arrived):
    return arrived[:, 1][:, :, None] * arrived[:, 0][:, None]


def finish(arrived):
    owners = lax.axis_size("tm") * lax.axis_size("band")
    my_rank = lax.axis_index("tm") * lax.axis_size("band") + lax.axis_index("band")
    q_local = arrived.shape[3]
    lane_width = arrived.shape[5]
    sample_total = SFT_DEV * owners * NB
    section_one = complex_einsum(
        "abqix,ic->abqcx", (arrived[:, :, 0], arrived[:, :, 1]), dft_table(owners, -1.0)
    )
    c_pos = lax.broadcasted_iota(jnp.int32, (owners, lane_width), 0)
    x_pos = lax.broadcasted_iota(jnp.int32, (owners, lane_width), 1)
    section_one = rotate(section_one, phase_pair(c_pos * (x_pos // NP), SFT_DEV * owners, -1.0))
    short_table = dft_table(SFT_DEV, -1.0)
    ident_rows = jnp.eye(NP, dtype=jnp.float32)
    spread = (jnp.kron(short_table[0], ident_rows), jnp.kron(short_table[1], ident_rows))
    section_two = complex_einsum("abqcx,xy->abqcy", section_one, spread)
    q_grid = my_rank * q_local + lax.broadcasted_iota(jnp.int32, (q_local, owners, lane_width), 0)
    c_grid = lax.broadcasted_iota(jnp.int32, (q_local, owners, lane_width), 1)
    x_grid = lax.broadcasted_iota(jnp.int32, (q_local, owners, lane_width), 2)
    time_index = x_grid % NP + NP * q_grid
    freq_index = c_grid + owners * (x_grid // NP)
    section_two = rotate(section_two, phase_pair(time_index * freq_index, sample_total, -1.0))
    packed = jnp.stack(section_two, axis=2)
    turned = lax.all_to_all(packed, ("tm", "band"), split_axis=4, concat_axis=3, tiled=True)
    turned = turned.reshape(turned.shape[0], 2, 2, NQ, lane_width)
    section_three = complex_einsum(
        "abqx,qv->abvx", (turned[:, :, 0], turned[:, :, 1]), dft_table(NQ, -1.0)
    )
    v_pos = lax.broadcasted_iota(jnp.int32, (NQ, lane_width), 0)
    p_pos = lax.broadcasted_iota(jnp.int32, (NQ, lane_width), 1) % NP
    section_three = rotate(section_three, phase_pair(v_pos * p_pos, NB, -1.0))
    fine_table = dft_table(NP, -1.0)
    ident_blocks = jnp.eye(SFT_DEV, dtype=jnp.float32)
    block_table = (jnp.kron(ident_blocks, fine_table[0]), jnp.kron(ident_blocks, fine_table[1]))
    result = complex_einsum("abvx,xy->abvy", section_three, block_table)
    return jnp.stack(result, axis=2)


def per_device(sft_bins, delay_code, antenna):
    owners = lax.axis_size("tm") * lax.axis_size("band")
    sample_total = SFT_DEV * owners * NB
    spectra = lax.all_to_all(sft_bins, "band", split_axis=1, concat_axis=2, tiled=True)
    bin_grid = spectra.reshape(2, SFT_DEV, NP, NQ)
    section_one = complex_einsum("pk,skl->spl", dft_table(NP, 1.0), (bin_grid[0], bin_grid[1]))
    p_rows = lax.broadcasted_iota(jnp.int32, (NP, NQ), 0)
    l_cols = lax.broadcasted_iota(jnp.int32, (NP, NQ), 1)
    section_one = rotate(section_one, phase_pair(p_rows * l_cols, NB, 1.0))
    series_pair = complex_einsum("spl,lq->spq", section_one, dft_table(NQ, 1.0))
    norm_scale = 1.0 / math.sqrt(NB)
    stacked = jnp.stack([series_pair[0] * norm_scale, series_pair[1] * norm_scale])
    rim_cols = (MAXD + 1 + NP) // NP
    head_rim = stacked[:, 0, :, :rim_cols]
    tail_rim = stacked[:, SFT_DEV - 1, :, NQ - rim_cols :]
    after_rim = shifted(head_rim, ("tm", "band"), -1)
    before = shifted(tail_rim, ("tm", "band"), 1)
    rim_size = NP * rim_cols
    span_len = SFT_DEV * NB
    timed = stacked.transpose(0, 1, 3, 2).reshape(2, span_len)
    before_timed = before.transpose(0, 2, 1).reshape(2, rim_size)
    after_timed = after_rim.transpose(0, 2, 1).reshape(2, rim_size)
    buffer = jnp.concatenate([before_timed, timed, after_timed], axis=1)
    lane_width = SFT_DEV * NP
    tmpl_local = delay_code.shape[0]
    run_count = span_len // RUN
    code_time = (
        delay_code.reshape(tmpl_local, NQ, SFT_DEV, NP)
        .transpose(0, 2, 1, 3)
        .reshape(tmpl_local, run_count, RUN)
    )
    offsets = code_time[:, :, 0] // NFRAC - MAXD
    run_starts = (jnp.arange(run_count, dtype=jnp.int32) * RUN)[None, :] + offsets + (rim_size - 1)

    def take_segment(start):
        return lax.dynamic_slice_in_dim(buffer, start, RUN + 3, 1)

    segments = jax.vmap(jax.vmap(take_segment))(run_starts)
    fraction = (code_time % NFRAC).astype(jnp.float32) / NFRAC
    coeffs = lagrange(fraction)
    res_time = coeffs[0][:, :, None, :] * segments[:, :, :, 0:RUN]
    for tap_index in range(1, 4):
        res_time = (
            res_time
            + coeffs[tap_index][:, :, None, :] * segments[:, :, :, tap_index : tap_index + RUN]
        )
    resampled = res_time.transpose(0, 2, 1, 3).reshape(tmpl_local, 2, SFT_DEV, NQ, NP)
    resampled = resampled.transpose(0, 1, 3, 2, 4).reshape(tmpl_local, 2, NQ, lane_width)
    weight_a = antenna[:, 0]
    weight_b = antenna[:, 1]
    local_sums = jnp.stack(
        [
            jnp.sum(weight_a * weight_a, axis=(1, 2)),
            jnp.sum(weight_b * weight_b, axis=(1, 2)),
            jnp.sum(weight_a * weight_b, axis=(1, 2)),
        ],
        axis=1,
    )
    totals = lax.psum(local_sums, ("tm", "band"))
    payload = jnp.stack([resampled, antenna], axis=1)
    spectra_out = finish(
        apply_weights(
            lax.all_to_all(
                payload[:, :, :, :, None, :],
                ("tm", "band"),
                split_axis=3,
                concat_axis=4,
                tiled=True,
            )
        )
    )
    out_scale = 1.0 / math.sqrt(sample_total)
    a_real = spectra_out[:, 0, 0] * out_scale
    a_imag = spectra_out[:, 0, 1] * out_scale
    b_real = spectra_out[:, 1, 0] * out_scale
    b_imag = spectra_out[:, 1, 1] * out_scale
    power_a = (totals[:, 0] / sample_total + stat_eps)[:, None, None]
    power_b = (totals[:, 1] / sample_total + stat_eps)[:, None, None]
    cross_ab = (totals[:, 2] / sample_total)[:, None, None]
    det_floor = jnp.maximum(
        power_a * power_b - cross_ab * cross_ab, floor_share * power_a * power_b
    )
    f_stat = (
        power_b * (a_real * a_real + a_imag * a_imag)
        + power_a * (b_real * b_real + b_imag * b_imag)
        - 2.0 * cross_ab * (a_real * b_real + a_imag * b_imag)
    ) / det_floor
    return f_stat[:, :, None, :]


LANES = 128
ROWS = 8
HALO = 2


def split_table(table):
    high = table.astype(jnp.bfloat16)
    low = (table - high.astype(np.float64)).astype(jnp.bfloat16)
    return np.stack([high, low])


def unit(product, modulus, sign):
    angle = sign * 2.0 * np.pi / modulus * (product % modulus)
    return np.cos(angle), np.sin(angle)


def inverse_tables():
    p_at = np.arange(NP)[:, None]
    l_at = np.arange(NQ)[None, :]
    twist = np.stack(unit(p_at * l_at, NB, 1.0)) / math.sqrt(NB)
    real, imag = unit(np.arange(NQ)[:, None] * l_at, NQ, 1.0)
    full = np.block([[real, -imag], [imag, real]])
    return twist.astype(np.float32), split_table(full)


def forward_table():
    lane = np.arange(LANES)
    bins = ROWS * (lane % NP) + lane // NP
    real, imag = unit(np.arange(LANES)[:, None] * bins[None, :], LANES, -1.0)
    return split_table(np.block([[real, imag], [-imag, real]]))


def add(one, two):
    return one[0] + two[0], one[1] + two[1]


def sub(one, two):
    return one[0] - two[0], one[1] - two[1]


def turn(value, step, length, sign):
    real, imag = value
    step = step % length
    if step == 0:
        return value
    if 2 * step == length:
        return -real, -imag
    if 4 * step == length:
        return (-imag, real) if sign > 0 else (imag, -real)
    if 4 * step == 3 * length:
        return (imag, -real) if sign > 0 else (-imag, real)
    angle = sign * 2.0 * math.pi * step / length
    cos_part, sin_part = math.cos(angle), math.sin(angle)
    if 8 * step == length:
        root = math.sqrt(0.5)
        if sign > 0:
            return (real - imag) * root, (real + imag) * root
        return (real + imag) * root, (imag - real) * root
    return real * cos_part - imag * sin_part, real * sin_part + imag * cos_part


def small_fft(values, sign):
    length = len(values)
    if length == 1:
        return values
    if length == 2:
        return [add(values[0], values[1]), sub(values[0], values[1])]
    even = small_fft(values[0::2], sign)
    odd = small_fft(values[1::2], sign)
    half = length // 2
    turned = [turn(odd[k], k, length, sign) for k in range(half)]
    return [add(even[k], turned[k]) for k in range(half)] + [sub(even[k], turned[k]) for k in range(half)]


def times(value, cos_part, sin_part):
    real, imag = value
    return real * cos_part - imag * sin_part, real * sin_part + imag * cos_part


def block_transposes(tiles):
    row = lax.broadcasted_iota(jnp.int32, (ROWS, LANES), 0)
    group = lax.broadcasted_iota(jnp.int32, (ROWS, LANES), 1) // NP
    gather_at = (group + row) & (ROWS - 1)
    reverse_at = (ROWS - row) & (ROWS - 1)
    tiles = [pltpu.roll(tile, 0, 1, stride=NP, stride_axis=0) for tile in tiles]
    tiles = [jnp.take_along_axis(tile, gather_at, axis=0) for tile in tiles]
    tiles = [pltpu.roll(tile, 0, 1, stride=NP, stride_axis=0) for tile in tiles]
    return [jnp.take_along_axis(tile, reverse_at, axis=0) for tile in tiles]


def split_dot(lhs, rhs, dims):
    out = None
    for one, two in ((0, 0), (0, 1), (1, 0)):
        part = lax.dot_general(lhs[one], rhs[two], dims, preferred_element_type=jnp.float32)
        out = part if out is None else out + part
    return out


def split_value(value):
    high = value.astype(jnp.bfloat16)
    return high, (value - high.astype(jnp.float32)).astype(jnp.bfloat16)


def prepare_kernel(code_ref, antenna_ref, fraction_ref, weights_ref, sums_ref, start_ref):
    tmpl_local = code_ref.shape[0]
    owners = code_ref.shape[1] // (2 * ROWS)
    lane = lax.broadcasted_iota(jnp.int32, (ROWS, LANES), 1)
    row = lax.broadcasted_iota(jnp.int32, (ROWS, LANES), 0)
    for t in range(tmpl_local):
        for h in range(2):
            codes = [code_ref[t, pl.ds(2 * ROWS * j + ROWS * h, ROWS), :] for j in range(owners)]
            turned = block_transposes(codes)
            if h == 0:
                starts = jnp.zeros((ROWS, LANES), jnp.int32)
                for j in range(owners):
                    starts = jnp.where(lane == j, jnp.broadcast_to(turned[j][:, 0:1], (ROWS, LANES)), starts)
                starts = starts // NFRAC - MAXD + (row * owners + lane) * RUN + (NB - 1)
                start_ref[pl.ds(t * ROWS, ROWS), :] = starts
            for j in range(owners):
                level = (turned[j] & (NFRAC - 1)).astype(jnp.float32) * (1.0 / NFRAC)
                fraction_ref[pl.ds((t * SFT_DEV * 2 + h) * ROWS + j, ROWS, stride=2 * ROWS), :] = level
        sums = [jnp.zeros((ROWS, LANES), jnp.float32) for _ in range(3)]
        for h in range(2):
            places = [pl.ds(2 * ROWS * j + ROWS * h, ROWS) for j in range(owners)]
            one = [antenna_ref[t, 0, place, :] for place in places]
            two = [antenna_ref[t, 1, place, :] for place in places]
            for first, second in zip(one, two):
                sums = [sums[0] + first * first, sums[1] + second * second, sums[2] + first * second]
            for w, tiles in ((0, one), (1, two)):
                turned = block_transposes(tiles)
                for j in range(owners):
                    at = ((t * 2 + w) * SFT_DEV * 2 + h) * ROWS + j
                    weights_ref[pl.ds(at, ROWS, stride=2 * ROWS), :] = turned[j]
        for index in range(3):
            sums_ref[pl.ds(t * 4 + index, 1), :] = jnp.sum(sums[index], axis=0, keepdims=True)
        sums_ref[pl.ds(t * 4 + 3, 1), :] = jnp.zeros((1, LANES), jnp.float32)


def resample_kernel(
    band_ref,
    start_in_ref,
    local_ref,
    far_ref,
    same_ref,
    other_ref,
    fraction_ref,
    weights_ref,
    sums_ref,
    twist_ref,
    table_ref,
    out_ref,
    z_ref,
    grid_ref,
    time_ref,
    run_ref,
    start_ref,
    copy_sem,
):
    starts_copy = pltpu.make_async_copy(start_in_ref, start_ref, copy_sem)
    starts_copy.start()
    band = band_ref[0]
    first = band == 0
    half = NP // 2
    owners = out_ref.shape[0]
    slot = out_ref.shape[1]
    tmpl_local = start_ref.shape[0] // SFT_DEV
    row = lax.broadcasted_iota(jnp.int32, (ROWS, LANES), 0)
    lane = lax.broadcasted_iota(jnp.int32, (ROWS, LANES), 1)
    for group in range(2):
        values = [[None, None] for _ in range(NP)]
        for part in range(2):
            for kappa in range(half):
                cols = pl.ds(LANES * kappa, LANES)
                if group == 0:
                    rows = pl.ds(pl.multiple_of(band * SFT_DEV, SFT_DEV), SFT_DEV)
                    mine = local_ref[part, rows, cols]
                    far = far_ref[part, rows, cols]
                else:
                    inner = [
                        jnp.where(first, ref[part, pl.ds(SFT_DEV, 1), cols], ref[part, pl.ds(SFT_DEV - 1, 1), cols])
                        for ref in (local_ref, far_ref)
                    ]
                    mine = jnp.where(row == 0, same_ref[part, :, cols], inner[0])
                    far = jnp.where(row == 0, other_ref[part, :, cols], inner[1])
                values[kappa][part] = jnp.where(first, mine, far)
                values[kappa + half][part] = jnp.where(first, far, mine)
        values = small_fft([tuple(value) for value in values], 1.0)
        for p in range(NP):
            turned = times(values[p], twist_ref[0, pl.ds(p, 1), :], twist_ref[1, pl.ds(p, 1), :])
            for part in range(2):
                z_ref[part, pl.ds(LANES * group + p, ROWS, stride=NP), :] = turned[part]
    dims = (((1,), (1,)), ((), ()))
    z_value = split_value(jnp.concatenate([z_ref[0], z_ref[1]], axis=1))
    grid_ref[...] = split_dot((table_ref[0], table_ref[1]), z_value, dims)
    per_sft = NB // LANES
    late_row = 2 * (per_sft // 2)
    early_row = 2 * per_sft * (SFT_DEV + 1)
    outer_row = jnp.where(first, late_row, early_row)
    inner_row = jnp.where(first, early_row, late_row)
    take_late = (lane < NP) == first
    for part in range(2):
        tiles = [grid_ref[pl.ds(NQ * part + ROWS * r, ROWS), pl.ds(0, LANES)] for r in range(per_sft)]
        tiles = block_transposes(tiles)
        for r in range(per_sft):
            time_ref[pl.ds(2 * (per_sft + r) + part, ROWS, stride=2 * per_sft), :] = tiles[r]
        tiles = [grid_ref[pl.ds(NQ * part + ROWS * r, ROWS), pl.ds(LANES, LANES)] for r in range(per_sft)]
        tiles = [jnp.where(take_late, tiles[r + per_sft // 2], tiles[r]) for r in range(per_sft // 2)]
        tiles = block_transposes(tiles)
        for r in range(per_sft // 2):
            time_ref[pl.ds(outer_row + 2 * r + part, 1), :] = tiles[r][0:1]
            time_ref[pl.ds(inner_row + 2 * r + part, 1), :] = tiles[r][1:2]
    for j in range(owners):
        out_ref[j, pl.ds(slot - ROWS, ROWS), :] = sums_ref[...]
    starts_copy.wait()
    flat_ref = out_ref.reshape(owners * slot, LANES)

    def one_sft(s_local, carry):
        for t in range(tmpl_local):
            starts = [start_ref[t * SFT_DEV + s_local, j] for j in range(owners)]
            shifts = [start & (LANES - 1) for start in starts]
            tiles = [time_ref[pl.ds((start >> 7) * 2, ROWS), :] for start in starts]
            tiles = [pltpu.roll(tile, (LANES - shift) & (LANES - 1), 1) for tile, shift in zip(tiles, shifts)]
            later = [pltpu.roll(tile, ROWS - 2, 0) for tile in tiles]
            for j in range(owners):
                run_ref[pl.ds((t * owners + j) * ROWS, ROWS), :] = jnp.where(
                    lane < LANES - shifts[j], tiles[j], later[j]
                )
        rows = [
            [
                [run_ref[pl.ds(t * owners * ROWS + 2 * i + part, ROWS, stride=ROWS), :] for i in range(3)]
                for part in range(2)
            ]
            for t in range(tmpl_local)
        ]
        for t in range(tmpl_local):
            at = (t * SFT_DEV + s_local) * 2
            coeffs = [lagrange(fraction_ref[pl.ds((at + h) * ROWS, ROWS), :]) for h in range(2)]
            weights = [
                [
                    weights_ref[pl.ds((((t * 2 + w) * SFT_DEV + s_local) * 2 + h) * ROWS, ROWS), :]
                    for h in range(2)
                ]
                for w in range(2)
            ]
            for part in range(2):
                totals = [coeffs[h][0] * rows[t][part][h] for h in range(2)]
                for k in range(1, 4):
                    rolled = [pltpu.roll(tile, LANES - k, 1) for tile in rows[t][part]]
                    for h in range(2):
                        tap = jnp.where(lane < LANES - k, rolled[h], rolled[h + 1])
                        totals[h] = totals[h] + coeffs[h][k] * tap
                for w in range(2):
                    for h in range(2):
                        at = (part * SFT_DEV + s_local) * ROWS + t * 4 + w * 2 + h
                        flat_ref[pl.ds(at, owners, stride=slot), :] = totals[h] * weights[w][h]
        return carry

    lax.fori_loop(0, SFT_DEV, one_sft, 0)


def section_kernel(samples_ref, out_ref, sums_ref, mid_ref):
    owners = samples_ref.shape[0]
    slot = samples_ref.shape[1]
    for s_local in range(SFT_DEV):
        values = [
            tuple(samples_ref[i, pl.ds((part * SFT_DEV + s_local) * ROWS, ROWS), :] for part in range(2))
            for i in range(owners)
        ]
        values = small_fft(values, -1.0)
        for c in range(owners):
            turned = turn(values[c], c * s_local, owners * SFT_DEV, -1.0)
            for part in range(2):
                mid_ref[part, pl.ds((c * SFT_DEV + s_local) * ROWS, ROWS), :] = turned[part]
    for c in range(owners):
        values = []
        for s_local in range(SFT_DEV):
            rows = pl.ds((c * SFT_DEV + s_local) * ROWS, ROWS)
            values.append((mid_ref[0, rows, :], mid_ref[1, rows, :]))
        values = small_fft(values, -1.0)
        for d in range(SFT_DEV):
            for part in range(2):
                out_ref[c, pl.ds(part * ROWS * ROWS + d, ROWS, stride=ROWS), :] = values[d][part]
    total = samples_ref[0, pl.ds(slot - ROWS, ROWS), :]
    for i in range(1, owners):
        total = total + samples_ref[i, pl.ds(slot - ROWS, ROWS), :]
    sums_ref[...] = jnp.broadcast_to(jnp.sum(total, axis=1, keepdims=True), (ROWS, LANES))


def statistic_kernel(sample_total, parts_ref, sums_ref, coarse_ref, fine_ref, table_ref, out_ref):
    rhs = (table_ref[0], table_ref[1])
    dims = (((1,), (0,)), ((), ()))
    tmpl_local = out_ref.shape[0]
    owners = parts_ref.shape[0]
    for t in range(tmpl_local):
        spectra = []
        for w in range(2):
            values = []
            for rho in range(2 * owners):
                j, h = rho // 2, rho % 2
                base = (t * 4 + w * 2 + h) * ROWS
                value = tuple(parts_ref[j, pl.ds(part * ROWS * ROWS + base, ROWS), :] for part in range(2))
                rows = pl.ds(rho * ROWS, ROWS)
                values.append(times(value, coarse_ref[0, rows, :], coarse_ref[1, rows, :]))
            values = small_fft(values, -1.0)
            values = [
                times(values[a], fine_ref[0, pl.ds(a * ROWS, ROWS), :], fine_ref[1, pl.ds(a * ROWS, ROWS), :])
                for a in range(2 * owners)
            ]
            real = jnp.concatenate([value[0] for value in values], axis=0)
            imag = jnp.concatenate([value[1] for value in values], axis=0)
            lhs = split_value(jnp.concatenate([real, imag], axis=1))
            out = split_dot(lhs, rhs, dims)
            spectra.append((out[:, :LANES], out[:, LANES:]))
        (a_real, a_imag), (b_real, b_imag) = spectra
        power_a = sums_ref[pl.ds(t * 4, 1), :] * (1.0 / sample_total) + stat_eps
        power_b = sums_ref[pl.ds(t * 4 + 1, 1), :] * (1.0 / sample_total) + stat_eps
        cross_ab = sums_ref[pl.ds(t * 4 + 2, 1), :] * (1.0 / sample_total)
        det_floor = jnp.maximum(power_a * power_b - cross_ab * cross_ab, floor_share * power_a * power_b)
        f_stat = (
            (power_b / det_floor) * (a_real * a_real + a_imag * a_imag)
            + (power_a / det_floor) * (b_real * b_real + b_imag * b_imag)
            - (2.0 * cross_ab / det_floor) * (a_real * b_real + a_imag * b_imag)
        )
        tiles = block_transposes([f_stat[a * ROWS : (a + 1) * ROWS] for a in range(2 * owners)])
        for a in range(2 * owners):
            out_ref[t, pl.ds(a, ROWS, stride=2 * owners), :] = tiles[a]


def vmem():
    return pl.BlockSpec(memory_space=pltpu.VMEM)


def resident(value):
    return pltpu.with_memory_space_constraint(value, pltpu.VMEM)


def exchange_bins(sft_bins):
    owner_count = lax.axis_size("tm") * lax.axis_size("band")
    first = lax.axis_index("band") == 0
    axes = ("tm", "band")
    straight, crossed = [], []
    for rank in range(owner_count):
        up = rank % 2 == 0
        target = rank + 2 if up else rank - 2
        if 0 <= target < owner_count:
            straight.append((rank, target))
        target = rank - 1 if up else rank + 1
        if 0 <= target < owner_count:
            crossed.append((rank, target))
    far = lax.ppermute(sft_bins, "band", [(0, 1), (1, 0)])
    tail, head = sft_bins[:, -1:], sft_bins[:, :1]
    same = lax.ppermute(jnp.where(first, tail, head), axes, straight)
    other = lax.ppermute(jnp.where(first, head, tail), axes, crossed)
    return far, same, other


def run_device(sft_bins, delay_code, antenna):
    axes = ("tm", "band")
    owners = lax.axis_size("tm") * lax.axis_size("band")
    my_rank = lax.axis_index("tm") * lax.axis_size("band") + lax.axis_index("band")
    sample_total = SFT_DEV * owners * NB
    tmpl_local = delay_code.shape[0]
    f32 = jnp.float32
    slot = SFT_DEV * ROWS
    far, same, other = exchange_bins(sft_bins)
    fraction, weights, sums, starts = pl.pallas_call(
        prepare_kernel,
        out_shape=(
            pltpu.VMEM((tmpl_local * SFT_DEV * 2 * ROWS, LANES), f32),
            pltpu.VMEM((tmpl_local * 2 * SFT_DEV * 2 * ROWS, LANES), f32),
            pltpu.VMEM((ROWS, LANES), f32),
            pltpu.VMEM((tmpl_local * SFT_DEV, LANES), jnp.int32),
        ),
        in_specs=[vmem(), vmem()],
        out_specs=(vmem(),) * 4,
        name="prepare",
    )(resident(delay_code), resident(antenna))
    twist, inverse_table = inverse_tables()
    band = lax.axis_index("band").astype(jnp.int32).reshape(1)
    operands = [starts, sft_bins, far, same, other, fraction, weights, sums, jnp.asarray(twist), jnp.asarray(inverse_table)]
    samples = pl.pallas_call(
        resample_kernel,
        out_shape=pltpu.VMEM((owners, 2 * slot + ROWS, LANES), f32),
        in_specs=[pl.BlockSpec(memory_space=pltpu.SMEM)] + [vmem()] * len(operands),
        out_specs=vmem(),
        scratch_shapes=[
            pltpu.VMEM((2, 2 * LANES, LANES), f32),
            pltpu.VMEM((2 * LANES, 2 * LANES), f32),
            pltpu.VMEM((2 * (SFT_DEV + 2) * NB // LANES, LANES), f32),
            pltpu.VMEM((tmpl_local * owners * ROWS, LANES), f32),
            pltpu.SMEM((tmpl_local * SFT_DEV, LANES), jnp.int32),
            pltpu.SemaphoreType.DMA,
        ],
        name="resample",
    )(band, *[resident(operand) for operand in operands])
    samples = lax.all_to_all(samples, axes, split_axis=0, concat_axis=0, tiled=True)
    parts, totals = pl.pallas_call(
        section_kernel,
        out_shape=(pltpu.VMEM((owners, 2 * slot, LANES), f32), pltpu.VMEM((ROWS, LANES), f32)),
        in_specs=[vmem()],
        out_specs=(vmem(), vmem()),
        scratch_shapes=[pltpu.VMEM((2, owners * slot, LANES), f32)],
        name="section",
    )(resident(samples))
    parts = lax.all_to_all(parts, axes, split_axis=0, concat_axis=0, tiled=True)
    row = lax.broadcasted_iota(jnp.int32, (2 * owners * ROWS, LANES), 0)
    lane = lax.broadcasted_iota(jnp.int32, (2 * owners * ROWS, LANES), 1)
    freq = my_rank + owners * (row % ROWS)
    coarse = jnp.stack(phase_pair((row // ROWS) * freq, sample_total // LANES, -1.0))
    fine = jnp.stack(phase_pair(lane * (freq + owners * SFT_DEV * (row // ROWS)), sample_total, -1.0))
    fine = fine * (1.0 / math.sqrt(sample_total))
    operands = [parts, totals, coarse, fine, jnp.asarray(forward_table())]
    f_stat = pl.pallas_call(
        functools.partial(statistic_kernel, sample_total),
        out_shape=jax.ShapeDtypeStruct((tmpl_local, NQ, LANES), f32),
        in_specs=[vmem()] * len(operands),
        out_specs=vmem(),
        name="statistic",
    )(*[resident(operand) for operand in operands])
    return f_stat[:, :, None, :]


def solution(mesh):
    owners = mesh.shape["tm"] * mesh.shape["band"]
    one_run_each = NB // RUN == owners and mesh.shape["band"] == 2
    in_specs = (
        P(None, ("groups", "tm"), "band"),
        P(("groups", "tmpl"), None, ("tm", "band")),
        P(("groups", "tmpl"), None, None, ("tm", "band")),
    )
    out_specs = P(("groups", "tmpl"), None, ("tm", "band"), None)
    return jax.shard_map(
        run_device if one_run_each else per_device,
        mesh=mesh,
        in_specs=in_specs,
        out_specs=out_specs,
        check_vma=False,
    )
```

```python
import functools
import math

import jax
import jax.numpy as jnp
import numpy as np
from jax import lax
from jax.experimental import pallas as pl
from jax.experimental.pallas import tpu as pltpu
from jax.sharding import PartitionSpec as P

NB = 2048
NQ = 128
NP = 16
SFT_DEV = 8
MAXD = 1000
NFRAC = 8
RUN = 256


stat_eps = 1e-06
floor_share = 0.5


def shifted(value, axis, by):
    length = lax.axis_size(axis)
    pairs = [(i, i + by) for i in range(length) if 0 <= i + by < length]
    return lax.ppermute(value, axis, pairs)


def lagrange(fraction):
    return (
        -fraction * (fraction - 1.0) * (fraction - 2.0) / 6.0,
        (fraction + 1.0) * (fraction - 1.0) * (fraction - 2.0) / 2.0,
        -(fraction + 1.0) * fraction * (fraction - 2.0) / 2.0,
        (fraction + 1.0) * fraction * (fraction - 1.0) / 6.0,
    )


def phase_pair(product, modulus, direction):
    angles = direction * 2.0 * math.pi / modulus * (product % modulus).astype(jnp.float32)
    return (jnp.cos(angles), jnp.sin(angles))


def dft_table(length, direction):
    rows_at = lax.broadcasted_iota(jnp.int32, (length, length), 0)
    cols_at = lax.broadcasted_iota(jnp.int32, (length, length), 1)
    return phase_pair(rows_at * cols_at, length, direction)


def complex_einsum(pattern, lhs_pair, rhs_pair):
    lhs_real, lhs_imag = lhs_pair
    rhs_real, rhs_imag = rhs_pair
    high = lax.Precision.HIGHEST
    out_real = jnp.einsum(pattern, lhs_real, rhs_real, precision=high) - jnp.einsum(
        pattern, lhs_imag, rhs_imag, precision=high
    )
    out_imag = jnp.einsum(pattern, lhs_real, rhs_imag, precision=high) + jnp.einsum(
        pattern, lhs_imag, rhs_real, precision=high
    )
    return (out_real, out_imag)


def rotate(values, phases):
    val_real, val_imag = values
    cos_part, sin_part = phases
    return (val_real * cos_part - val_imag * sin_part, val_real * sin_part + val_imag * cos_part)


def apply_weights(arrived):
    return arrived[:, 1][:, :, None] * arrived[:, 0][:, None]


def finish(arrived):
    owners = lax.axis_size("tm") * lax.axis_size("band")
    my_rank = lax.axis_index("tm") * lax.axis_size("band") + lax.axis_index("band")
    q_local = arrived.shape[3]
    lane_width = arrived.shape[5]
    sample_total = SFT_DEV * owners * NB
    section_one = complex_einsum(
        "abqix,ic->abqcx", (arrived[:, :, 0], arrived[:, :, 1]), dft_table(owners, -1.0)
    )
    c_pos = lax.broadcasted_iota(jnp.int32, (owners, lane_width), 0)
    x_pos = lax.broadcasted_iota(jnp.int32, (owners, lane_width), 1)
    section_one = rotate(section_one, phase_pair(c_pos * (x_pos // NP), SFT_DEV * owners, -1.0))
    short_table = dft_table(SFT_DEV, -1.0)
    ident_rows = jnp.eye(NP, dtype=jnp.float32)
    spread = (jnp.kron(short_table[0], ident_rows), jnp.kron(short_table[1], ident_rows))
    section_two = complex_einsum("abqcx,xy->abqcy", section_one, spread)
    q_grid = my_rank * q_local + lax.broadcasted_iota(jnp.int32, (q_local, owners, lane_width), 0)
    c_grid = lax.broadcasted_iota(jnp.int32, (q_local, owners, lane_width), 1)
    x_grid = lax.broadcasted_iota(jnp.int32, (q_local, owners, lane_width), 2)
    time_index = x_grid % NP + NP * q_grid
    freq_index = c_grid + owners * (x_grid // NP)
    section_two = rotate(section_two, phase_pair(time_index * freq_index, sample_total, -1.0))
    packed = jnp.stack(section_two, axis=2)
    turned = lax.all_to_all(packed, ("tm", "band"), split_axis=4, concat_axis=3, tiled=True)
    turned = turned.reshape(turned.shape[0], 2, 2, NQ, lane_width)
    section_three = complex_einsum(
        "abqx,qv->abvx", (turned[:, :, 0], turned[:, :, 1]), dft_table(NQ, -1.0)
    )
    v_pos = lax.broadcasted_iota(jnp.int32, (NQ, lane_width), 0)
    p_pos = lax.broadcasted_iota(jnp.int32, (NQ, lane_width), 1) % NP
    section_three = rotate(section_three, phase_pair(v_pos * p_pos, NB, -1.0))
    fine_table = dft_table(NP, -1.0)
    ident_blocks = jnp.eye(SFT_DEV, dtype=jnp.float32)
    block_table = (jnp.kron(ident_blocks, fine_table[0]), jnp.kron(ident_blocks, fine_table[1]))
    result = complex_einsum("abvx,xy->abvy", section_three, block_table)
    return jnp.stack(result, axis=2)


def per_device(sft_bins, delay_code, antenna):
    owners = lax.axis_size("tm") * lax.axis_size("band")
    sample_total = SFT_DEV * owners * NB
    spectra = lax.all_to_all(sft_bins, "band", split_axis=1, concat_axis=2, tiled=True)
    bin_grid = spectra.reshape(2, SFT_DEV, NP, NQ)
    section_one = complex_einsum("pk,skl->spl", dft_table(NP, 1.0), (bin_grid[0], bin_grid[1]))
    p_rows = lax.broadcasted_iota(jnp.int32, (NP, NQ), 0)
    l_cols = lax.broadcasted_iota(jnp.int32, (NP, NQ), 1)
    section_one = rotate(section_one, phase_pair(p_rows * l_cols, NB, 1.0))
    series_pair = complex_einsum("spl,lq->spq", section_one, dft_table(NQ, 1.0))
    norm_scale = 1.0 / math.sqrt(NB)
    stacked = jnp.stack([series_pair[0] * norm_scale, series_pair[1] * norm_scale])
    rim_cols = (MAXD + 1 + NP) // NP
    head_rim = stacked[:, 0, :, :rim_cols]
    tail_rim = stacked[:, SFT_DEV - 1, :, NQ - rim_cols :]
    after_rim = shifted(head_rim, ("tm", "band"), -1)
    before = shifted(tail_rim, ("tm", "band"), 1)
    rim_size = NP * rim_cols
    span_len = SFT_DEV * NB
    timed = stacked.transpose(0, 1, 3, 2).reshape(2, span_len)
    before_timed = before.transpose(0, 2, 1).reshape(2, rim_size)
    after_timed = after_rim.transpose(0, 2, 1).reshape(2, rim_size)
    buffer = jnp.concatenate([before_timed, timed, after_timed], axis=1)
    lane_width = SFT_DEV * NP
    tmpl_local = delay_code.shape[0]
    run_count = span_len // RUN
    code_time = (
        delay_code.reshape(tmpl_local, NQ, SFT_DEV, NP)
        .transpose(0, 2, 1, 3)
        .reshape(tmpl_local, run_count, RUN)
    )
    offsets = code_time[:, :, 0] // NFRAC - MAXD
    run_starts = (jnp.arange(run_count, dtype=jnp.int32) * RUN)[None, :] + offsets + (rim_size - 1)

    def take_segment(start):
        return lax.dynamic_slice_in_dim(buffer, start, RUN + 3, 1)

    segments = jax.vmap(jax.vmap(take_segment))(run_starts)
    fraction = (code_time % NFRAC).astype(jnp.float32) / NFRAC
    coeffs = lagrange(fraction)
    res_time = coeffs[0][:, :, None, :] * segments[:, :, :, 0:RUN]
    for tap_index in range(1, 4):
        res_time = (
            res_time
            + coeffs[tap_index][:, :, None, :] * segments[:, :, :, tap_index : tap_index + RUN]
        )
    resampled = res_time.transpose(0, 2, 1, 3).reshape(tmpl_local, 2, SFT_DEV, NQ, NP)
    resampled = resampled.transpose(0, 1, 3, 2, 4).reshape(tmpl_local, 2, NQ, lane_width)
    weight_a = antenna[:, 0]
    weight_b = antenna[:, 1]
    local_sums = jnp.stack(
        [
            jnp.sum(weight_a * weight_a, axis=(1, 2)),
            jnp.sum(weight_b * weight_b, axis=(1, 2)),
            jnp.sum(weight_a * weight_b, axis=(1, 2)),
        ],
        axis=1,
    )
    totals = lax.psum(local_sums, ("tm", "band"))
    payload = jnp.stack([resampled, antenna], axis=1)
    spectra_out = finish(
        apply_weights(
            lax.all_to_all(
                payload[:, :, :, :, None, :],
                ("tm", "band"),
                split_axis=3,
                concat_axis=4,
                tiled=True,
            )
        )
    )
    out_scale = 1.0 / math.sqrt(sample_total)
    a_real = spectra_out[:, 0, 0] * out_scale
    a_imag = spectra_out[:, 0, 1] * out_scale
    b_real = spectra_out[:, 1, 0] * out_scale
    b_imag = spectra_out[:, 1, 1] * out_scale
    power_a = (totals[:, 0] / sample_total + stat_eps)[:, None, None]
    power_b = (totals[:, 1] / sample_total + stat_eps)[:, None, None]
    cross_ab = (totals[:, 2] / sample_total)[:, None, None]
    det_floor = jnp.maximum(
        power_a * power_b - cross_ab * cross_ab, floor_share * power_a * power_b
    )
    f_stat = (
        power_b * (a_real * a_real + a_imag * a_imag)
        + power_a * (b_real * b_real + b_imag * b_imag)
        - 2.0 * cross_ab * (a_real * b_real + a_imag * b_imag)
    ) / det_floor
    return f_stat[:, :, None, :]


LANES = 128
ROWS = 8
HALO = 2


def split_table(table):
    high = table.astype(jnp.bfloat16)
    low = (table - high.astype(np.float64)).astype(jnp.bfloat16)
    return np.stack([high, low])


def unit(product, modulus, sign):
    angle = sign * 2.0 * np.pi / modulus * (product % modulus)
    return np.cos(angle), np.sin(angle)


def inverse_tables():
    p_at = np.arange(NP)[:, None]
    l_at = np.arange(NQ)[None, :]
    twist = np.stack(unit(p_at * l_at, NB, 1.0)) / math.sqrt(NB)
    real, imag = unit(np.arange(NQ)[:, None] * l_at, NQ, 1.0)
    full = np.block([[real, -imag], [imag, real]])
    return twist.astype(np.float32), split_table(full)


def forward_table():
    lane = np.arange(LANES)
    bins = ROWS * (lane % NP) + lane // NP
    real, imag = unit(np.arange(LANES)[:, None] * bins[None, :], LANES, -1.0)
    return split_table(np.block([[real, imag], [-imag, real]]))


def add(one, two):
    return one[0] + two[0], one[1] + two[1]


def sub(one, two):
    return one[0] - two[0], one[1] - two[1]


def turn(value, step, length, sign):
    real, imag = value
    step = step % length
    if step == 0:
        return value
    if 2 * step == length:
        return -real, -imag
    if 4 * step == length:
        return (-imag, real) if sign > 0 else (imag, -real)
    if 4 * step == 3 * length:
        return (imag, -real) if sign > 0 else (-imag, real)
    angle = sign * 2.0 * math.pi * step / length
    cos_part, sin_part = math.cos(angle), math.sin(angle)
    if 8 * step == length:
        root = math.sqrt(0.5)
        if sign > 0:
            return (real - imag) * root, (real + imag) * root
        return (real + imag) * root, (imag - real) * root
    return real * cos_part - imag * sin_part, real * sin_part + imag * cos_part


def small_fft(values, sign):
    length = len(values)
    if length == 1:
        return values
    if length == 2:
        return [add(values[0], values[1]), sub(values[0], values[1])]
    even = small_fft(values[0::2], sign)
    odd = small_fft(values[1::2], sign)
    half = length // 2
    turned = [turn(odd[k], k, length, sign) for k in range(half)]
    return [add(even[k], turned[k]) for k in range(half)] + [sub(even[k], turned[k]) for k in range(half)]


def times(value, cos_part, sin_part):
    real, imag = value
    return real * cos_part - imag * sin_part, real * sin_part + imag * cos_part


def block_transposes(tiles):
    row = lax.broadcasted_iota(jnp.int32, (ROWS, LANES), 0)
    group = lax.broadcasted_iota(jnp.int32, (ROWS, LANES), 1) // NP
    gather_at = (group + row) & (ROWS - 1)
    reverse_at = (ROWS - row) & (ROWS - 1)
    tiles = [pltpu.roll(tile, 0, 1, stride=NP, stride_axis=0) for tile in tiles]
    tiles = [jnp.take_along_axis(tile, gather_at, axis=0) for tile in tiles]
    tiles = [pltpu.roll(tile, 0, 1, stride=NP, stride_axis=0) for tile in tiles]
    return [jnp.take_along_axis(tile, reverse_at, axis=0) for tile in tiles]


def split_dot(lhs, rhs, dims):
    out = None
    for one, two in ((0, 0), (0, 1), (1, 0)):
        part = lax.dot_general(lhs[one], rhs[two], dims, preferred_element_type=jnp.float32)
        out = part if out is None else out + part
    return out


def split_value(value):
    high = value.astype(jnp.bfloat16)
    return high, (value - high.astype(jnp.float32)).astype(jnp.bfloat16)


def prepare_kernel(code_ref, antenna_ref, bins_ref, fraction_ref, weights_ref, sums_ref, start_ref, mine_ref):
    mine_ref[...] = bins_ref[...]
    tmpl_local = code_ref.shape[0]
    owners = code_ref.shape[1] // (2 * ROWS)
    lane = lax.broadcasted_iota(jnp.int32, (ROWS, LANES), 1)
    row = lax.broadcasted_iota(jnp.int32, (ROWS, LANES), 0)
    for t in range(tmpl_local):
        for h in range(2):
            codes = [code_ref[t, pl.ds(2 * ROWS * j + ROWS * h, ROWS), :] for j in range(owners)]
            turned = block_transposes(codes)
            if h == 0:
                starts = jnp.zeros((ROWS, LANES), jnp.int32)
                for j in range(owners):
                    starts = jnp.where(lane == j, jnp.broadcast_to(turned[j][:, 0:1], (ROWS, LANES)), starts)
                starts = starts // NFRAC - MAXD + (row * owners + lane) * RUN + (NB - 1)
                start_ref[pl.ds(t * ROWS, ROWS), :] = starts
            for j in range(owners):
                level = (turned[j] & (NFRAC - 1)).astype(jnp.float32) * (1.0 / NFRAC)
                fraction_ref[pl.ds((t * SFT_DEV * 2 + h) * ROWS + j, ROWS, stride=2 * ROWS), :] = level
        sums = [jnp.zeros((ROWS, LANES), jnp.float32) for _ in range(3)]
        for h in range(2):
            places = [pl.ds(2 * ROWS * j + ROWS * h, ROWS) for j in range(owners)]
            one = [antenna_ref[t, 0, place, :] for place in places]
            two = [antenna_ref[t, 1, place, :] for place in places]
            for first, second in zip(one, two):
                sums = [sums[0] + first * first, sums[1] + second * second, sums[2] + first * second]
            for w, tiles in ((0, one), (1, two)):
                turned = block_transposes(tiles)
                for j in range(owners):
                    at = ((t * 2 + w) * SFT_DEV * 2 + h) * ROWS + j
                    weights_ref[pl.ds(at, ROWS, stride=2 * ROWS), :] = turned[j]
        for index in range(3):
            sums_ref[pl.ds(t * 4 + index, 1), :] = jnp.sum(sums[index], axis=0, keepdims=True)
        sums_ref[pl.ds(t * 4 + 3, 1), :] = jnp.zeros((1, LANES), jnp.float32)


def pack_kernel(band_ref, mine_ref, far_ref, out_ref):
    first = band_ref[0] == 0
    half = NP // 2
    last = mine_ref.shape[1] - 1
    for part in range(2):
        for kappa in range(half):
            cols = pl.ds(LANES * kappa, LANES)
            mine, far = [
                jnp.where(first, ref[part, pl.ds(last, 1), cols], ref[part, pl.ds(0, 1), cols])
                for ref in (mine_ref, far_ref)
            ]
            out_ref[part, pl.ds(kappa, 1), :] = jnp.where(first, mine, far)
            out_ref[part, pl.ds(kappa + half, 1), :] = jnp.where(first, far, mine)


def inverse_columns(values, twist_ref, z_ref, places):
    values = small_fft(values, 1.0)
    for p in range(NP):
        turned = times(values[p], twist_ref[0, pl.ds(p, 1), :], twist_ref[1, pl.ds(p, 1), :])
        for part in range(2):
            z_ref[part, places[p], :] = turned[part]


def inverse_grid(table_ref, z_ref):
    z_value = split_value(jnp.concatenate([z_ref[0], z_ref[1]], axis=1))
    return split_dot((table_ref[0], table_ref[1]), z_value, (((1,), (1,)), ((), ())))


def halo_rows(grid, part, late):
    per_sft = NB // LANES
    tiles = [grid[NQ * part + ROWS * r : NQ * part + ROWS * (r + 1)] for r in range(per_sft)]
    tiles = [jnp.where(late, tiles[r + per_sft // 2], tiles[r]) for r in range(per_sft // 2)]
    return [tile[0:1] for tile in block_transposes(tiles)]


def late_row():
    return NB // LANES


def early_row():
    return 2 * (NB // LANES) * (SFT_DEV + 1)


def series_kernel(band_ref, mine_ref, far_ref, twist_ref, table_ref, time_ref, z_ref):
    band = band_ref[0]
    first = band == 0
    half = NP // 2
    per_sft = NB // LANES
    own = [[None, None] for _ in range(NP)]
    inner = [[None, None] for _ in range(NP)]
    for part in range(2):
        for kappa in range(half):
            cols = pl.ds(LANES * kappa, LANES)
            rows = pl.ds(pl.multiple_of(band * SFT_DEV, SFT_DEV), SFT_DEV)
            mine, far = mine_ref[part, rows, cols], far_ref[part, rows, cols]
            own[kappa][part] = jnp.where(first, mine, far)
            own[kappa + half][part] = jnp.where(first, far, mine)
            mine, far = [
                jnp.where(first, ref[part, pl.ds(SFT_DEV, 1), cols], ref[part, pl.ds(SFT_DEV - 1, 1), cols])
                for ref in (mine_ref, far_ref)
            ]
            inner[kappa][part] = jnp.where(first, mine, far)
            inner[kappa + half][part] = jnp.where(first, far, mine)
    inverse_columns([tuple(v) for v in own], twist_ref, z_ref, [pl.ds(p, ROWS, stride=NP) for p in range(NP)])
    inverse_columns([tuple(v) for v in inner], twist_ref, z_ref, [pl.ds(LANES + p, 1) for p in range(NP)])
    z_ref[:, pl.ds(LANES + NP, LANES - NP), :] = jnp.zeros((2, LANES - NP, LANES), jnp.float32)
    grid = inverse_grid(table_ref, z_ref)
    inner_row = jnp.where(first, early_row(), late_row())
    for part in range(2):
        tiles = [grid[NQ * part + ROWS * r : NQ * part + ROWS * (r + 1), :LANES] for r in range(per_sft)]
        tiles = block_transposes(tiles)
        for r in range(per_sft):
            time_ref[pl.ds(2 * (per_sft + r) + part, ROWS, stride=2 * per_sft), :] = tiles[r]
        tiles = halo_rows(grid[:, LANES:], part, jnp.logical_not(first))
        for r in range(per_sft // 2):
            time_ref[pl.ds(inner_row + 2 * r + part, 1), :] = tiles[r]


def resample_kernel(
    band_ref,
    start_in_ref,
    series_ref,
    outer_ref,
    fraction_ref,
    weights_ref,
    sums_ref,
    twist_ref,
    table_ref,
    out_ref,
    z_ref,
    time_ref,
    run_ref,
    start_ref,
    copy_sem,
):
    starts_copy = pltpu.make_async_copy(start_in_ref, start_ref, copy_sem)
    starts_copy.start()
    first = band_ref[0] == 0
    owners = out_ref.shape[0]
    slot = out_ref.shape[1]
    tmpl_local = start_ref.shape[0] // SFT_DEV
    lane = lax.broadcasted_iota(jnp.int32, (ROWS, LANES), 1)
    values = [tuple(outer_ref[part, pl.ds(kappa, 1), :] for part in range(2)) for kappa in range(NP)]
    z_ref[:, pl.ds(NP, LANES - NP), :] = jnp.zeros((2, LANES - NP, LANES), jnp.float32)
    inverse_columns(values, twist_ref, z_ref, [pl.ds(p, 1) for p in range(NP)])
    grid = inverse_grid(table_ref, z_ref)
    time_ref[...] = series_ref[...]
    outer_row = jnp.where(first, late_row(), early_row())
    for part in range(2):
        tiles = halo_rows(grid, part, first)
        for r in range(NB // LANES // 2):
            time_ref[pl.ds(outer_row + 2 * r + part, 1), :] = tiles[r]
    for j in range(owners):
        out_ref[j, pl.ds(slot - ROWS, ROWS), :] = sums_ref[...]
    starts_copy.wait()
    flat_ref = out_ref.reshape(owners * slot, LANES)

    def one_sft(s_local, carry):
        for t in range(tmpl_local):
            starts = [start_ref[t * SFT_DEV + s_local, j] for j in range(owners)]
            shifts = [start & (LANES - 1) for start in starts]
            tiles = [time_ref[pl.ds((start >> 7) * 2, ROWS), :] for start in starts]
            tiles = [pltpu.roll(tile, (LANES - shift) & (LANES - 1), 1) for tile, shift in zip(tiles, shifts)]
            later = [pltpu.roll(tile, ROWS - 2, 0) for tile in tiles]
            for j in range(owners):
                run_ref[pl.ds((t * owners + j) * ROWS, ROWS), :] = jnp.where(
                    lane < LANES - shifts[j], tiles[j], later[j]
                )
        rows = [
            [
                [run_ref[pl.ds(t * owners * ROWS + 2 * i + part, ROWS, stride=ROWS), :] for i in range(3)]
                for part in range(2)
            ]
            for t in range(tmpl_local)
        ]
        for t in range(tmpl_local):
            at = (t * SFT_DEV + s_local) * 2
            coeffs = [lagrange(fraction_ref[pl.ds((at + h) * ROWS, ROWS), :]) for h in range(2)]
            weights = [
                [
                    weights_ref[pl.ds((((t * 2 + w) * SFT_DEV + s_local) * 2 + h) * ROWS, ROWS), :]
                    for h in range(2)
                ]
                for w in range(2)
            ]
            for part in range(2):
                totals = [coeffs[h][0] * rows[t][part][h] for h in range(2)]
                for k in range(1, 4):
                    rolled = [pltpu.roll(tile, LANES - k, 1) for tile in rows[t][part]]
                    for h in range(2):
                        tap = jnp.where(lane < LANES - k, rolled[h], rolled[h + 1])
                        totals[h] = totals[h] + coeffs[h][k] * tap
                for w in range(2):
                    for h in range(2):
                        at = (part * SFT_DEV + s_local) * ROWS + t * 4 + w * 2 + h
                        flat_ref[pl.ds(at, owners, stride=slot), :] = totals[h] * weights[w][h]
        return carry

    lax.fori_loop(0, SFT_DEV, one_sft, 0)


def section_kernel(samples_ref, out_ref, sums_ref, mid_ref):
    owners = samples_ref.shape[0]
    slot = samples_ref.shape[1]
    for s_local in range(SFT_DEV):
        values = [
            tuple(samples_ref[i, pl.ds((part * SFT_DEV + s_local) * ROWS, ROWS), :] for part in range(2))
            for i in range(owners)
        ]
        values = small_fft(values, -1.0)
        for c in range(owners):
            turned = turn(values[c], c * s_local, owners * SFT_DEV, -1.0)
            for part in range(2):
                mid_ref[part, pl.ds((c * SFT_DEV + s_local) * ROWS, ROWS), :] = turned[part]
    for c in range(owners):
        values = []
        for s_local in range(SFT_DEV):
            rows = pl.ds((c * SFT_DEV + s_local) * ROWS, ROWS)
            values.append((mid_ref[0, rows, :], mid_ref[1, rows, :]))
        values = small_fft(values, -1.0)
        for d in range(SFT_DEV):
            for part in range(2):
                out_ref[c, pl.ds(part * ROWS * ROWS + d, ROWS, stride=ROWS), :] = values[d][part]
    total = samples_ref[0, pl.ds(slot - ROWS, ROWS), :]
    for i in range(1, owners):
        total = total + samples_ref[i, pl.ds(slot - ROWS, ROWS), :]
    sums_ref[...] = jnp.broadcast_to(jnp.sum(total, axis=1, keepdims=True), (ROWS, LANES))


def statistic_kernel(sample_total, parts_ref, sums_ref, coarse_ref, fine_ref, table_ref, out_ref):
    rhs = (table_ref[0], table_ref[1])
    dims = (((1,), (0,)), ((), ()))
    tmpl_local = out_ref.shape[0]
    owners = parts_ref.shape[0]
    for t in range(tmpl_local):
        spectra = []
        for w in range(2):
            values = []
            for rho in range(2 * owners):
                j, h = rho // 2, rho % 2
                base = (t * 4 + w * 2 + h) * ROWS
                value = tuple(parts_ref[j, pl.ds(part * ROWS * ROWS + base, ROWS), :] for part in range(2))
                rows = pl.ds(rho * ROWS, ROWS)
                values.append(times(value, coarse_ref[0, rows, :], coarse_ref[1, rows, :]))
            values = small_fft(values, -1.0)
            values = [
                times(values[a], fine_ref[0, pl.ds(a * ROWS, ROWS), :], fine_ref[1, pl.ds(a * ROWS, ROWS), :])
                for a in range(2 * owners)
            ]
            real = jnp.concatenate([value[0] for value in values], axis=0)
            imag = jnp.concatenate([value[1] for value in values], axis=0)
            lhs = split_value(jnp.concatenate([real, imag], axis=1))
            out = split_dot(lhs, rhs, dims)
            spectra.append((out[:, :LANES], out[:, LANES:]))
        (a_real, a_imag), (b_real, b_imag) = spectra
        power_a = sums_ref[pl.ds(t * 4, 1), :] * (1.0 / sample_total) + stat_eps
        power_b = sums_ref[pl.ds(t * 4 + 1, 1), :] * (1.0 / sample_total) + stat_eps
        cross_ab = sums_ref[pl.ds(t * 4 + 2, 1), :] * (1.0 / sample_total)
        det_floor = jnp.maximum(power_a * power_b - cross_ab * cross_ab, floor_share * power_a * power_b)
        f_stat = (
            (power_b / det_floor) * (a_real * a_real + a_imag * a_imag)
            + (power_a / det_floor) * (b_real * b_real + b_imag * b_imag)
            - (2.0 * cross_ab / det_floor) * (a_real * b_real + a_imag * b_imag)
        )
        tiles = block_transposes([f_stat[a * ROWS : (a + 1) * ROWS] for a in range(2 * owners)])
        for a in range(2 * owners):
            out_ref[t, pl.ds(a, ROWS, stride=2 * owners), :] = tiles[a]


def vmem():
    return pl.BlockSpec(memory_space=pltpu.VMEM)


def resident(value):
    return pltpu.with_memory_space_constraint(value, pltpu.VMEM)


def run_device(sft_bins, delay_code, antenna):
    axes = ("tm", "band")
    owners = lax.axis_size("tm") * lax.axis_size("band")
    my_rank = lax.axis_index("tm") * lax.axis_size("band") + lax.axis_index("band")
    sample_total = SFT_DEV * owners * NB
    tmpl_local = delay_code.shape[0]
    f32 = jnp.float32
    slot = SFT_DEV * ROWS
    time_rows = 2 * (SFT_DEV + 2) * NB // LANES
    smem = pl.BlockSpec(memory_space=pltpu.SMEM)
    band = lax.axis_index("band").astype(jnp.int32).reshape(1)
    far = lax.ppermute(sft_bins, "band", [(0, 1), (1, 0)])
    fraction, weights, sums, starts, mine = pl.pallas_call(
        prepare_kernel,
        out_shape=(
            pltpu.VMEM((tmpl_local * SFT_DEV * 2 * ROWS, LANES), f32),
            pltpu.VMEM((tmpl_local * 2 * SFT_DEV * 2 * ROWS, LANES), f32),
            pltpu.VMEM((ROWS, LANES), f32),
            pltpu.VMEM((tmpl_local * SFT_DEV, LANES), jnp.int32),
            pltpu.VMEM(sft_bins.shape, f32),
        ),
        in_specs=[vmem()] * 3,
        out_specs=(vmem(),) * 5,
        name="prepare",
    )(delay_code, antenna, sft_bins)
    far, mine = resident(far), resident(mine)
    edge = pl.pallas_call(
        pack_kernel,
        out_shape=pltpu.VMEM((2, NP, LANES), f32),
        in_specs=[smem, vmem(), vmem()],
        out_specs=vmem(),
        name="pack",
    )(band, mine, far)
    along = [(rank, rank + 2) for rank in range(0, owners - 2, 2)]
    along += [(rank, rank - 2) for rank in range(3, owners, 2)]
    outer = lax.ppermute(edge, axes, along)
    twist, inverse_table = [resident(jnp.asarray(table)) for table in inverse_tables()]
    series = pl.pallas_call(
        series_kernel,
        out_shape=pltpu.VMEM((time_rows, LANES), f32),
        in_specs=[smem] + [vmem()] * 4,
        out_specs=vmem(),
        scratch_shapes=[pltpu.VMEM((2, 2 * LANES, LANES), f32)],
        name="series",
    )(band, mine, far, twist, inverse_table)
    operands = [resident(value) for value in (starts, series, outer, fraction, weights, sums)]
    operands += [twist, inverse_table]
    samples = pl.pallas_call(
        resample_kernel,
        out_shape=pltpu.VMEM((owners, 2 * slot + ROWS, LANES), f32),
        in_specs=[smem] + [vmem()] * len(operands),
        out_specs=vmem(),
        scratch_shapes=[
            pltpu.VMEM((2, LANES, LANES), f32),
            pltpu.VMEM((time_rows, LANES), f32),
            pltpu.VMEM((tmpl_local * owners * ROWS, LANES), f32),
            pltpu.SMEM((tmpl_local * SFT_DEV, LANES), jnp.int32),
            pltpu.SemaphoreType.DMA,
        ],
        name="resample",
    )(band, *operands)
    samples = lax.all_to_all(samples, axes, split_axis=0, concat_axis=0, tiled=True)
    parts, totals = pl.pallas_call(
        section_kernel,
        out_shape=(pltpu.VMEM((owners, 2 * slot, LANES), f32), pltpu.VMEM((ROWS, LANES), f32)),
        in_specs=[vmem()],
        out_specs=(vmem(), vmem()),
        scratch_shapes=[pltpu.VMEM((2, owners * slot, LANES), f32)],
        name="section",
    )(resident(samples))
    parts = lax.all_to_all(parts, axes, split_axis=0, concat_axis=0, tiled=True)
    row = lax.broadcasted_iota(jnp.int32, (2 * owners * ROWS, LANES), 0)
    lane = lax.broadcasted_iota(jnp.int32, (2 * owners * ROWS, LANES), 1)
    freq = my_rank + owners * (row % ROWS)
    coarse = jnp.stack(phase_pair((row // ROWS) * freq, sample_total // LANES, -1.0))
    fine = jnp.stack(phase_pair(lane * (freq + owners * SFT_DEV * (row // ROWS)), sample_total, -1.0))
    fine = fine * (1.0 / math.sqrt(sample_total))
    operands = [parts, totals, coarse, fine, jnp.asarray(forward_table())]
    f_stat = pl.pallas_call(
        functools.partial(statistic_kernel, sample_total),
        out_shape=jax.ShapeDtypeStruct((tmpl_local, NQ, LANES), f32),
        in_specs=[vmem()] * len(operands),
        out_specs=vmem(),
        name="statistic",
    )(*[resident(operand) for operand in operands])
    return f_stat[:, :, None, :]


def solution(mesh):
    owners = mesh.shape["tm"] * mesh.shape["band"]
    one_run_each = NB // RUN == owners and mesh.shape["band"] == 2
    in_specs = (
        P(None, ("groups", "tm"), "band"),
        P(("groups", "tmpl"), None, ("tm", "band")),
        P(("groups", "tmpl"), None, None, ("tm", "band")),
    )
    out_specs = P(("groups", "tmpl"), None, ("tm", "band"), None)
    return jax.shard_map(
        run_device if one_run_each else per_device,
        mesh=mesh,
        in_specs=in_specs,
        out_specs=out_specs,
        check_vma=False,
    )
```

```python
import functools
import math

import jax
import jax.numpy as jnp
import numpy as np
from jax import lax
from jax.experimental import pallas as pl
from jax.experimental.pallas import tpu as pltpu
from jax.sharding import PartitionSpec as P

NB = 2048
NQ = 128
NP = 16
SFT_DEV = 8
MAXD = 1000
NFRAC = 8
RUN = 256


stat_eps = 1e-06
floor_share = 0.5


def shifted(value, axis, by):
    length = lax.axis_size(axis)
    pairs = [(i, i + by) for i in range(length) if 0 <= i + by < length]
    return lax.ppermute(value, axis, pairs)


def lagrange(fraction):
    return (
        -fraction * (fraction - 1.0) * (fraction - 2.0) / 6.0,
        (fraction + 1.0) * (fraction - 1.0) * (fraction - 2.0) / 2.0,
        -(fraction + 1.0) * fraction * (fraction - 2.0) / 2.0,
        (fraction + 1.0) * fraction * (fraction - 1.0) / 6.0,
    )


def phase_pair(product, modulus, direction):
    angles = direction * 2.0 * math.pi / modulus * (product % modulus).astype(jnp.float32)
    return (jnp.cos(angles), jnp.sin(angles))


def dft_table(length, direction):
    rows_at = lax.broadcasted_iota(jnp.int32, (length, length), 0)
    cols_at = lax.broadcasted_iota(jnp.int32, (length, length), 1)
    return phase_pair(rows_at * cols_at, length, direction)


def complex_einsum(pattern, lhs_pair, rhs_pair):
    lhs_real, lhs_imag = lhs_pair
    rhs_real, rhs_imag = rhs_pair
    high = lax.Precision.HIGHEST
    out_real = jnp.einsum(pattern, lhs_real, rhs_real, precision=high) - jnp.einsum(
        pattern, lhs_imag, rhs_imag, precision=high
    )
    out_imag = jnp.einsum(pattern, lhs_real, rhs_imag, precision=high) + jnp.einsum(
        pattern, lhs_imag, rhs_real, precision=high
    )
    return (out_real, out_imag)


def rotate(values, phases):
    val_real, val_imag = values
    cos_part, sin_part = phases
    return (val_real * cos_part - val_imag * sin_part, val_real * sin_part + val_imag * cos_part)


def apply_weights(arrived):
    return arrived[:, 1][:, :, None] * arrived[:, 0][:, None]


def finish(arrived):
    owners = lax.axis_size("tm") * lax.axis_size("band")
    my_rank = lax.axis_index("tm") * lax.axis_size("band") + lax.axis_index("band")
    q_local = arrived.shape[3]
    lane_width = arrived.shape[5]
    sample_total = SFT_DEV * owners * NB
    section_one = complex_einsum(
        "abqix,ic->abqcx", (arrived[:, :, 0], arrived[:, :, 1]), dft_table(owners, -1.0)
    )
    c_pos = lax.broadcasted_iota(jnp.int32, (owners, lane_width), 0)
    x_pos = lax.broadcasted_iota(jnp.int32, (owners, lane_width), 1)
    section_one = rotate(section_one, phase_pair(c_pos * (x_pos // NP), SFT_DEV * owners, -1.0))
    short_table = dft_table(SFT_DEV, -1.0)
    ident_rows = jnp.eye(NP, dtype=jnp.float32)
    spread = (jnp.kron(short_table[0], ident_rows), jnp.kron(short_table[1], ident_rows))
    section_two = complex_einsum("abqcx,xy->abqcy", section_one, spread)
    q_grid = my_rank * q_local + lax.broadcasted_iota(jnp.int32, (q_local, owners, lane_width), 0)
    c_grid = lax.broadcasted_iota(jnp.int32, (q_local, owners, lane_width), 1)
    x_grid = lax.broadcasted_iota(jnp.int32, (q_local, owners, lane_width), 2)
    time_index = x_grid % NP + NP * q_grid
    freq_index = c_grid + owners * (x_grid // NP)
    section_two = rotate(section_two, phase_pair(time_index * freq_index, sample_total, -1.0))
    packed = jnp.stack(section_two, axis=2)
    turned = lax.all_to_all(packed, ("tm", "band"), split_axis=4, concat_axis=3, tiled=True)
    turned = turned.reshape(turned.shape[0], 2, 2, NQ, lane_width)
    section_three = complex_einsum(
        "abqx,qv->abvx", (turned[:, :, 0], turned[:, :, 1]), dft_table(NQ, -1.0)
    )
    v_pos = lax.broadcasted_iota(jnp.int32, (NQ, lane_width), 0)
    p_pos = lax.broadcasted_iota(jnp.int32, (NQ, lane_width), 1) % NP
    section_three = rotate(section_three, phase_pair(v_pos * p_pos, NB, -1.0))
    fine_table = dft_table(NP, -1.0)
    ident_blocks = jnp.eye(SFT_DEV, dtype=jnp.float32)
    block_table = (jnp.kron(ident_blocks, fine_table[0]), jnp.kron(ident_blocks, fine_table[1]))
    result = complex_einsum("abvx,xy->abvy", section_three, block_table)
    return jnp.stack(result, axis=2)


def per_device(sft_bins, delay_code, antenna):
    owners = lax.axis_size("tm") * lax.axis_size("band")
    sample_total = SFT_DEV * owners * NB
    spectra = lax.all_to_all(sft_bins, "band", split_axis=1, concat_axis=2, tiled=True)
    bin_grid = spectra.reshape(2, SFT_DEV, NP, NQ)
    section_one = complex_einsum("pk,skl->spl", dft_table(NP, 1.0), (bin_grid[0], bin_grid[1]))
    p_rows = lax.broadcasted_iota(jnp.int32, (NP, NQ), 0)
    l_cols = lax.broadcasted_iota(jnp.int32, (NP, NQ), 1)
    section_one = rotate(section_one, phase_pair(p_rows * l_cols, NB, 1.0))
    series_pair = complex_einsum("spl,lq->spq", section_one, dft_table(NQ, 1.0))
    norm_scale = 1.0 / math.sqrt(NB)
    stacked = jnp.stack([series_pair[0] * norm_scale, series_pair[1] * norm_scale])
    rim_cols = (MAXD + 1 + NP) // NP
    head_rim = stacked[:, 0, :, :rim_cols]
    tail_rim = stacked[:, SFT_DEV - 1, :, NQ - rim_cols :]
    after_rim = shifted(head_rim, ("tm", "band"), -1)
    before = shifted(tail_rim, ("tm", "band"), 1)
    rim_size = NP * rim_cols
    span_len = SFT_DEV * NB
    timed = stacked.transpose(0, 1, 3, 2).reshape(2, span_len)
    before_timed = before.transpose(0, 2, 1).reshape(2, rim_size)
    after_timed = after_rim.transpose(0, 2, 1).reshape(2, rim_size)
    buffer = jnp.concatenate([before_timed, timed, after_timed], axis=1)
    lane_width = SFT_DEV * NP
    tmpl_local = delay_code.shape[0]
    run_count = span_len // RUN
    code_time = (
        delay_code.reshape(tmpl_local, NQ, SFT_DEV, NP)
        .transpose(0, 2, 1, 3)
        .reshape(tmpl_local, run_count, RUN)
    )
    offsets = code_time[:, :, 0] // NFRAC - MAXD
    run_starts = (jnp.arange(run_count, dtype=jnp.int32) * RUN)[None, :] + offsets + (rim_size - 1)

    def take_segment(start):
        return lax.dynamic_slice_in_dim(buffer, start, RUN + 3, 1)

    segments = jax.vmap(jax.vmap(take_segment))(run_starts)
    fraction = (code_time % NFRAC).astype(jnp.float32) / NFRAC
    coeffs = lagrange(fraction)
    res_time = coeffs[0][:, :, None, :] * segments[:, :, :, 0:RUN]
    for tap_index in range(1, 4):
        res_time = (
            res_time
            + coeffs[tap_index][:, :, None, :] * segments[:, :, :, tap_index : tap_index + RUN]
        )
    resampled = res_time.transpose(0, 2, 1, 3).reshape(tmpl_local, 2, SFT_DEV, NQ, NP)
    resampled = resampled.transpose(0, 1, 3, 2, 4).reshape(tmpl_local, 2, NQ, lane_width)
    weight_a = antenna[:, 0]
    weight_b = antenna[:, 1]
    local_sums = jnp.stack(
        [
            jnp.sum(weight_a * weight_a, axis=(1, 2)),
            jnp.sum(weight_b * weight_b, axis=(1, 2)),
            jnp.sum(weight_a * weight_b, axis=(1, 2)),
        ],
        axis=1,
    )
    totals = lax.psum(local_sums, ("tm", "band"))
    payload = jnp.stack([resampled, antenna], axis=1)
    spectra_out = finish(
        apply_weights(
            lax.all_to_all(
                payload[:, :, :, :, None, :],
                ("tm", "band"),
                split_axis=3,
                concat_axis=4,
                tiled=True,
            )
        )
    )
    out_scale = 1.0 / math.sqrt(sample_total)
    a_real = spectra_out[:, 0, 0] * out_scale
    a_imag = spectra_out[:, 0, 1] * out_scale
    b_real = spectra_out[:, 1, 0] * out_scale
    b_imag = spectra_out[:, 1, 1] * out_scale
    power_a = (totals[:, 0] / sample_total + stat_eps)[:, None, None]
    power_b = (totals[:, 1] / sample_total + stat_eps)[:, None, None]
    cross_ab = (totals[:, 2] / sample_total)[:, None, None]
    det_floor = jnp.maximum(
        power_a * power_b - cross_ab * cross_ab, floor_share * power_a * power_b
    )
    f_stat = (
        power_b * (a_real * a_real + a_imag * a_imag)
        + power_a * (b_real * b_real + b_imag * b_imag)
        - 2.0 * cross_ab * (a_real * b_real + a_imag * b_imag)
    ) / det_floor
    return f_stat[:, :, None, :]


LANES = 128
ROWS = 8
HALO = 2


def split_table(table):
    high = table.astype(jnp.bfloat16)
    low = (table - high.astype(np.float64)).astype(jnp.bfloat16)
    return np.stack([high, low])


def unit(product, modulus, sign):
    angle = sign * 2.0 * np.pi / modulus * (product % modulus)
    return np.cos(angle), np.sin(angle)


def inverse_tables():
    p_at = np.arange(NP)[:, None]
    l_at = np.arange(NQ)[None, :]
    twist = np.stack(unit(p_at * l_at, NB, 1.0)) / math.sqrt(NB)
    real, imag = unit(np.arange(NQ)[:, None] * l_at, NQ, 1.0)
    full = np.block([[real, -imag], [imag, real]])
    return twist.astype(np.float32), split_table(full)


def forward_table():
    lane = np.arange(LANES)
    bins = ROWS * (lane % NP) + lane // NP
    real, imag = unit(np.arange(LANES)[:, None] * bins[None, :], LANES, -1.0)
    return split_table(np.block([[real, imag], [-imag, real]]))


def add(one, two):
    return one[0] + two[0], one[1] + two[1]


def sub(one, two):
    return one[0] - two[0], one[1] - two[1]


def turn(value, step, length, sign):
    real, imag = value
    step = step % length
    if step == 0:
        return value
    if 2 * step == length:
        return -real, -imag
    if 4 * step == length:
        return (-imag, real) if sign > 0 else (imag, -real)
    if 4 * step == 3 * length:
        return (imag, -real) if sign > 0 else (-imag, real)
    angle = sign * 2.0 * math.pi * step / length
    cos_part, sin_part = math.cos(angle), math.sin(angle)
    if 8 * step == length:
        root = math.sqrt(0.5)
        if sign > 0:
            return (real - imag) * root, (real + imag) * root
        return (real + imag) * root, (imag - real) * root
    return real * cos_part - imag * sin_part, real * sin_part + imag * cos_part


def small_fft(values, sign):
    length = len(values)
    if length == 1:
        return values
    if length == 2:
        return [add(values[0], values[1]), sub(values[0], values[1])]
    even = small_fft(values[0::2], sign)
    odd = small_fft(values[1::2], sign)
    half = length // 2
    turned = [turn(odd[k], k, length, sign) for k in range(half)]
    return [add(even[k], turned[k]) for k in range(half)] + [sub(even[k], turned[k]) for k in range(half)]


def times(value, cos_part, sin_part):
    real, imag = value
    return real * cos_part - imag * sin_part, real * sin_part + imag * cos_part


def block_transposes(tiles):
    row = lax.broadcasted_iota(jnp.int32, (ROWS, LANES), 0)
    group = lax.broadcasted_iota(jnp.int32, (ROWS, LANES), 1) // NP
    gather_at = (group + row) & (ROWS - 1)
    reverse_at = (ROWS - row) & (ROWS - 1)
    tiles = [pltpu.roll(tile, 0, 1, stride=NP, stride_axis=0) for tile in tiles]
    tiles = [jnp.take_along_axis(tile, gather_at, axis=0) for tile in tiles]
    tiles = [pltpu.roll(tile, 0, 1, stride=NP, stride_axis=0) for tile in tiles]
    return [jnp.take_along_axis(tile, reverse_at, axis=0) for tile in tiles]


def split_dot(lhs, rhs, dims):
    out = None
    for one, two in ((0, 0), (0, 1), (1, 0)):
        part = lax.dot_general(lhs[one], rhs[two], dims, preferred_element_type=jnp.float32)
        out = part if out is None else out + part
    return out


def split_value(value):
    high = value.astype(jnp.bfloat16)
    return high, (value - high.astype(jnp.float32)).astype(jnp.bfloat16)


def prepare_kernel(code_ref, antenna_ref, bins_ref, fraction_ref, weights_ref, sums_ref, start_ref, shift_ref, mine_ref):
    mine_ref[...] = bins_ref[...]
    tmpl_local = code_ref.shape[0]
    owners = code_ref.shape[1] // (2 * ROWS)
    lane = lax.broadcasted_iota(jnp.int32, (ROWS, LANES), 1)
    row = lax.broadcasted_iota(jnp.int32, (ROWS, LANES), 0)
    for t in range(tmpl_local):
        for h in range(2):
            codes = [code_ref[t, pl.ds(2 * ROWS * j + ROWS * h, ROWS), :] for j in range(owners)]
            turned = block_transposes(codes)
            if h == 0:
                starts = jnp.zeros((ROWS, LANES), jnp.int32)
                for j in range(owners):
                    whole = jnp.broadcast_to(turned[j][:, 0:1], (ROWS, LANES)) // NFRAC - MAXD
                    start = whole + (row * owners + j) * RUN + (NB - 1)
                    starts = jnp.where(lane == j, start, starts)
                    shift_ref[pl.ds(t * SFT_DEV * owners + j, ROWS, stride=owners), :] = start & (LANES - 1)
                start_ref[pl.ds(t * ROWS, ROWS), :] = starts
            for j in range(owners):
                level = (turned[j] & (NFRAC - 1)).astype(jnp.float32) * (1.0 / NFRAC)
                fraction_ref[pl.ds((t * SFT_DEV * 2 + h) * ROWS + j, ROWS, stride=2 * ROWS), :] = level
        sums = [jnp.zeros((ROWS, LANES), jnp.float32) for _ in range(3)]
        for h in range(2):
            places = [pl.ds(2 * ROWS * j + ROWS * h, ROWS) for j in range(owners)]
            one = [antenna_ref[t, 0, place, :] for place in places]
            two = [antenna_ref[t, 1, place, :] for place in places]
            for first, second in zip(one, two):
                sums = [sums[0] + first * first, sums[1] + second * second, sums[2] + first * second]
            for w, tiles in ((0, one), (1, two)):
                turned = block_transposes(tiles)
                for j in range(owners):
                    at = ((t * 2 + w) * SFT_DEV * 2 + h) * ROWS + j
                    weights_ref[pl.ds(at, ROWS, stride=2 * ROWS), :] = turned[j]
        for index in range(3):
            sums_ref[pl.ds(t * 4 + index, 1), :] = jnp.sum(sums[index], axis=0, keepdims=True)
        sums_ref[pl.ds(t * 4 + 3, 1), :] = jnp.zeros((1, LANES), jnp.float32)


def pack_kernel(band_ref, mine_ref, far_ref, out_ref):
    first = band_ref[0] == 0
    half = NP // 2
    last = mine_ref.shape[1] - 1
    for part in range(2):
        for kappa in range(half):
            cols = pl.ds(LANES * kappa, LANES)
            mine, far = [
                jnp.where(first, ref[part, pl.ds(last, 1), cols], ref[part, pl.ds(0, 1), cols])
                for ref in (mine_ref, far_ref)
            ]
            out_ref[part, pl.ds(kappa, 1), :] = jnp.where(first, mine, far)
            out_ref[part, pl.ds(kappa + half, 1), :] = jnp.where(first, far, mine)


def inverse_columns(values, twist_ref, z_ref, places):
    values = small_fft(values, 1.0)
    for p in range(NP):
        turned = times(values[p], twist_ref[0, pl.ds(p, 1), :], twist_ref[1, pl.ds(p, 1), :])
        for part in range(2):
            z_ref[part, places[p], :] = turned[part]


def inverse_grid(table_ref, z_ref):
    z_value = split_value(jnp.concatenate([z_ref[0], z_ref[1]], axis=1))
    return split_dot((table_ref[0], table_ref[1]), z_value, (((1,), (1,)), ((), ())))


def halo_rows(grid, part, late):
    per_sft = NB // LANES
    tiles = [grid[NQ * part + ROWS * r : NQ * part + ROWS * (r + 1)] for r in range(per_sft)]
    tiles = [jnp.where(late, tiles[r + per_sft // 2], tiles[r]) for r in range(per_sft // 2)]
    return [tile[0:1] for tile in block_transposes(tiles)]


def late_row():
    return NB // LANES


def early_row():
    return 2 * (NB // LANES) * (SFT_DEV + 1)


def align_runs(time_ref, start_ref, run_ref, s_local, place):
    tmpl_local = start_ref.shape[0] // SFT_DEV
    owners = NB // RUN
    starts = [start_ref[t * SFT_DEV + s_local, j] for t in range(tmpl_local) for j in range(owners)]
    tiles = [time_ref[pl.ds((start >> 7) * 2, ROWS), :] for start in starts]
    tiles = [pltpu.roll(tile, (-start) & (LANES - 1), 1) for tile, start in zip(tiles, starts)]
    for at, tile in enumerate(tiles):
        run_ref[pl.ds((place * len(tiles) + at) * ROWS, ROWS), :] = tile


def combine_runs(run_ref, shift_ref, fraction_ref, weights_ref, flat_ref, slot, s_local, place):
    tmpl_local = shift_ref.shape[0] // (SFT_DEV * ROWS)
    owners = NB // RUN
    lane = lax.broadcasted_iota(jnp.int32, (ROWS, LANES), 1)

    def rows_at(group):
        return pl.ds(group * ROWS if isinstance(group, int) else pl.multiple_of(group * ROWS, ROWS), ROWS)

    for t in range(tmpl_local):
        straight = lane < LANES - shift_ref[rows_at(t * SFT_DEV + s_local), :]
        rows = []
        for part in range(2):
            base = (place * tmpl_local + t) * owners * ROWS + part
            raw = [run_ref[pl.ds(base + 2 * i, ROWS, stride=ROWS), :] for i in range(4)]
            rows.append([jnp.where(straight, raw[i], raw[i + 1]) for i in range(3)])
        at = (t * SFT_DEV + s_local) * 2
        coeffs = [lagrange(fraction_ref[rows_at(at + h), :]) for h in range(2)]
        totals = [[coeffs[h][0] * rows[part][h] for h in range(2)] for part in range(2)]
        for k in range(1, 4):
            rolled = [[pltpu.roll(tile, LANES - k, 1) for tile in rows[part]] for part in range(2)]
            for part in range(2):
                for h in range(2):
                    tap = jnp.where(lane < LANES - k, rolled[part][h], rolled[part][h + 1])
                    totals[part][h] = totals[part][h] + coeffs[h][k] * tap
        for w in range(2):
            at = ((t * 2 + w) * SFT_DEV + s_local) * 2
            for h in range(2):
                weight = weights_ref[rows_at(at + h), :]
                for part in range(2):
                    to = (part * SFT_DEV + s_local) * ROWS + t * 4 + w * 2 + h
                    flat_ref[pl.ds(to, owners, stride=slot), :] = totals[part][h] * weight


def series_kernel(
    band_ref,
    mine_ref,
    far_ref,
    twist_ref,
    table_ref,
    start_in_ref,
    shift_ref,
    fraction_ref,
    weights_ref,
    sums_ref,
    time_ref,
    out_ref,
    z_ref,
    run_ref,
    start_ref,
    copy_sem,
):
    starts_copy = pltpu.make_async_copy(start_in_ref, start_ref, copy_sem)
    starts_copy.start()
    owners, slot = out_ref.shape[:2]
    band = band_ref[0]
    first = band == 0
    half = NP // 2
    per_sft = NB // LANES
    own = [[None, None] for _ in range(NP)]
    inner = [[None, None] for _ in range(NP)]
    for part in range(2):
        for kappa in range(half):
            cols = pl.ds(LANES * kappa, LANES)
            rows = pl.ds(pl.multiple_of(band * SFT_DEV, SFT_DEV), SFT_DEV)
            mine, far = mine_ref[part, rows, cols], far_ref[part, rows, cols]
            own[kappa][part] = jnp.where(first, mine, far)
            own[kappa + half][part] = jnp.where(first, far, mine)
            mine, far = [
                jnp.where(first, ref[part, pl.ds(SFT_DEV, 1), cols], ref[part, pl.ds(SFT_DEV - 1, 1), cols])
                for ref in (mine_ref, far_ref)
            ]
            inner[kappa][part] = jnp.where(first, mine, far)
            inner[kappa + half][part] = jnp.where(first, far, mine)
    inverse_columns([tuple(v) for v in own], twist_ref, z_ref, [pl.ds(p, ROWS, stride=NP) for p in range(NP)])
    inverse_columns([tuple(v) for v in inner], twist_ref, z_ref, [pl.ds(LANES + p, 1) for p in range(NP)])
    z_ref[:, pl.ds(LANES + NP, LANES - NP), :] = jnp.zeros((2, LANES - NP, LANES), jnp.float32)
    grid = inverse_grid(table_ref, z_ref)
    inner_row = jnp.where(first, early_row(), late_row())
    for part in range(2):
        tiles = [grid[NQ * part + ROWS * r : NQ * part + ROWS * (r + 1), :LANES] for r in range(per_sft)]
        tiles = block_transposes(tiles)
        for r in range(per_sft):
            time_ref[pl.ds(2 * (per_sft + r) + part, ROWS, stride=2 * per_sft), :] = tiles[r]
        tiles = halo_rows(grid[:, LANES:], part, jnp.logical_not(first))
        for r in range(per_sft // 2):
            time_ref[pl.ds(inner_row + 2 * r + part, 1), :] = tiles[r]


    for j in range(owners):
        out_ref[j, pl.ds(slot - ROWS, ROWS), :] = sums_ref[...]
    starts_copy.wait()
    flat_ref = out_ref.reshape(owners * slot, LANES)
    order = list(range(1, SFT_DEV - 1)) + [jnp.where(first, SFT_DEV - 1, 0)]
    for place, s_local in enumerate(order):
        align_runs(time_ref, start_ref, run_ref, s_local, place)
    for place, s_local in enumerate(order):
        combine_runs(run_ref, shift_ref, fraction_ref, weights_ref, flat_ref, slot, s_local, place)


def resample_kernel(
    band_ref,
    start_in_ref,
    series_ref,
    outer_ref,
    shift_ref,
    fraction_ref,
    weights_ref,
    twist_ref,
    table_ref,
    partial_ref,
    out_ref,
    z_ref,
    time_ref,
    run_ref,
    start_ref,
    copy_sem,
):
    starts_copy = pltpu.make_async_copy(start_in_ref, start_ref, copy_sem)
    starts_copy.start()
    first = band_ref[0] == 0
    owners, slot = out_ref.shape[:2]
    values = [tuple(outer_ref[part, pl.ds(kappa, 1), :] for part in range(2)) for kappa in range(NP)]
    z_ref[:, pl.ds(NP, LANES - NP), :] = jnp.zeros((2, LANES - NP, LANES), jnp.float32)
    inverse_columns(values, twist_ref, z_ref, [pl.ds(p, 1) for p in range(NP)])
    grid = inverse_grid(table_ref, z_ref)
    time_ref[...] = series_ref[...]
    outer_row = jnp.where(first, late_row(), early_row())
    for part in range(2):
        tiles = halo_rows(grid, part, first)
        for r in range(NB // LANES // 2):
            time_ref[pl.ds(outer_row + 2 * r + part, 1), :] = tiles[r]
    starts_copy.wait()
    flat_ref = out_ref.reshape(owners * slot, LANES)
    s_local = jnp.where(first, 0, SFT_DEV - 1)
    align_runs(time_ref, start_ref, run_ref, s_local, 0)
    combine_runs(run_ref, shift_ref, fraction_ref, weights_ref, flat_ref, slot, s_local, 0)


def section_kernel(samples_ref, out_ref, sums_ref, mid_ref):
    owners = samples_ref.shape[0]
    slot = samples_ref.shape[1]
    for s_local in range(SFT_DEV):
        values = [
            tuple(samples_ref[i, pl.ds((part * SFT_DEV + s_local) * ROWS, ROWS), :] for part in range(2))
            for i in range(owners)
        ]
        values = small_fft(values, -1.0)
        for c in range(owners):
            turned = turn(values[c], c * s_local, owners * SFT_DEV, -1.0)
            for part in range(2):
                mid_ref[part, pl.ds((c * SFT_DEV + s_local) * ROWS, ROWS), :] = turned[part]
    for c in range(owners):
        values = []
        for s_local in range(SFT_DEV):
            rows = pl.ds((c * SFT_DEV + s_local) * ROWS, ROWS)
            values.append((mid_ref[0, rows, :], mid_ref[1, rows, :]))
        values = small_fft(values, -1.0)
        for d in range(SFT_DEV):
            for part in range(2):
                out_ref[c, pl.ds(part * ROWS * ROWS + d, ROWS, stride=ROWS), :] = values[d][part]
    total = samples_ref[0, pl.ds(slot - ROWS, ROWS), :]
    for i in range(1, owners):
        total = total + samples_ref[i, pl.ds(slot - ROWS, ROWS), :]
    sums_ref[...] = jnp.broadcast_to(jnp.sum(total, axis=1, keepdims=True), (ROWS, LANES))


def statistic_kernel(sample_total, parts_ref, sums_ref, coarse_ref, fine_ref, table_ref, out_ref):
    rhs = (table_ref[0], table_ref[1])
    dims = (((1,), (0,)), ((), ()))
    tmpl_local = out_ref.shape[0]
    owners = parts_ref.shape[0]
    for t in range(tmpl_local):
        spectra = []
        for w in range(2):
            values = []
            for rho in range(2 * owners):
                j, h = rho // 2, rho % 2
                base = (t * 4 + w * 2 + h) * ROWS
                value = tuple(parts_ref[j, pl.ds(part * ROWS * ROWS + base, ROWS), :] for part in range(2))
                rows = pl.ds(rho * ROWS, ROWS)
                values.append(times(value, coarse_ref[0, rows, :], coarse_ref[1, rows, :]))
            values = small_fft(values, -1.0)
            values = [
                times(values[a], fine_ref[0, pl.ds(a * ROWS, ROWS), :], fine_ref[1, pl.ds(a * ROWS, ROWS), :])
                for a in range(2 * owners)
            ]
            real = jnp.concatenate([value[0] for value in values], axis=0)
            imag = jnp.concatenate([value[1] for value in values], axis=0)
            lhs = split_value(jnp.concatenate([real, imag], axis=1))
            out = split_dot(lhs, rhs, dims)
            spectra.append((out[:, :LANES], out[:, LANES:]))
        (a_real, a_imag), (b_real, b_imag) = spectra
        power_a = sums_ref[pl.ds(t * 4, 1), :] * (1.0 / sample_total) + stat_eps
        power_b = sums_ref[pl.ds(t * 4 + 1, 1), :] * (1.0 / sample_total) + stat_eps
        cross_ab = sums_ref[pl.ds(t * 4 + 2, 1), :] * (1.0 / sample_total)
        det_floor = jnp.maximum(power_a * power_b - cross_ab * cross_ab, floor_share * power_a * power_b)
        f_stat = (
            (power_b / det_floor) * (a_real * a_real + a_imag * a_imag)
            + (power_a / det_floor) * (b_real * b_real + b_imag * b_imag)
            - (2.0 * cross_ab / det_floor) * (a_real * b_real + a_imag * b_imag)
        )
        tiles = block_transposes([f_stat[a * ROWS : (a + 1) * ROWS] for a in range(2 * owners)])
        for a in range(2 * owners):
            out_ref[t, pl.ds(a, ROWS, stride=2 * owners), :] = tiles[a]


def vmem():
    return pl.BlockSpec(memory_space=pltpu.VMEM)


def resident(value):
    return pltpu.with_memory_space_constraint(value, pltpu.VMEM)


def run_device(sft_bins, delay_code, antenna):
    axes = ("tm", "band")
    owners = lax.axis_size("tm") * lax.axis_size("band")
    my_rank = lax.axis_index("tm") * lax.axis_size("band") + lax.axis_index("band")
    sample_total = SFT_DEV * owners * NB
    tmpl_local = delay_code.shape[0]
    f32 = jnp.float32
    slot = SFT_DEV * ROWS
    time_rows = 2 * (SFT_DEV + 2) * NB // LANES
    smem = pl.BlockSpec(memory_space=pltpu.SMEM)
    band = lax.axis_index("band").astype(jnp.int32).reshape(1)
    far = lax.ppermute(sft_bins, "band", [(0, 1), (1, 0)])
    fraction, weights, sums, starts, shifts, mine = pl.pallas_call(
        prepare_kernel,
        out_shape=(
            pltpu.VMEM((tmpl_local * SFT_DEV * 2 * ROWS, LANES), f32),
            pltpu.VMEM((tmpl_local * 2 * SFT_DEV * 2 * ROWS, LANES), f32),
            pltpu.VMEM((ROWS, LANES), f32),
            pltpu.VMEM((tmpl_local * SFT_DEV, LANES), jnp.int32),
            pltpu.VMEM((tmpl_local * SFT_DEV * owners, LANES), jnp.int32),
            pltpu.VMEM(sft_bins.shape, f32),
        ),
        in_specs=[vmem()] * 3,
        out_specs=(vmem(),) * 6,
        name="prepare",
    )(delay_code, antenna, sft_bins)
    far, mine = resident(far), resident(mine)
    edge = pl.pallas_call(
        pack_kernel,
        out_shape=pltpu.VMEM((2, NP, LANES), f32),
        in_specs=[smem, vmem(), vmem()],
        out_specs=vmem(),
        name="pack",
    )(band, mine, far)
    along = [(rank, rank + 2) for rank in range(0, owners - 2, 2)]
    along += [(rank, rank - 2) for rank in range(3, owners, 2)]
    outer = lax.ppermute(edge, axes, along)
    twist, inverse_table = [resident(jnp.asarray(table)) for table in inverse_tables()]
    fraction, weights, sums, starts, shifts = [
        resident(value) for value in (fraction, weights, sums, starts, shifts)
    ]
    payload = pltpu.VMEM((owners, 2 * slot + ROWS, LANES), f32)
    scratch = [
        pltpu.SMEM((tmpl_local * SFT_DEV, LANES), jnp.int32),
        pltpu.SemaphoreType.DMA,
    ]
    series, partial = pl.pallas_call(
        series_kernel,
        out_shape=(pltpu.VMEM((time_rows, LANES), f32), payload),
        in_specs=[smem] + [vmem()] * 9,
        out_specs=(vmem(), vmem()),
        scratch_shapes=[
            pltpu.VMEM((2, 2 * LANES, LANES), f32),
            pltpu.VMEM(((SFT_DEV - 1) * tmpl_local * owners * ROWS, LANES), f32),
        ]
        + scratch,
        name="series",
    )(band, mine, far, twist, inverse_table, starts, shifts, fraction, weights, sums)
    operands = [starts, resident(series), resident(outer), shifts, fraction, weights, twist, inverse_table]
    operands += [resident(partial)]
    samples = pl.pallas_call(
        resample_kernel,
        out_shape=payload,
        in_specs=[smem] + [vmem()] * len(operands),
        out_specs=vmem(),
        scratch_shapes=[
            pltpu.VMEM((2, LANES, LANES), f32),
            pltpu.VMEM((time_rows, LANES), f32),
            pltpu.VMEM((tmpl_local * owners * ROWS, LANES), f32),
        ]
        + scratch,
        input_output_aliases={len(operands): 0},
        name="resample",
    )(band, *operands)
    samples = lax.all_to_all(samples, axes, split_axis=0, concat_axis=0, tiled=True)
    parts, totals = pl.pallas_call(
        section_kernel,
        out_shape=(pltpu.VMEM((owners, 2 * slot, LANES), f32), pltpu.VMEM((ROWS, LANES), f32)),
        in_specs=[vmem()],
        out_specs=(vmem(), vmem()),
        scratch_shapes=[pltpu.VMEM((2, owners * slot, LANES), f32)],
        name="section",
    )(resident(samples))
    parts = lax.all_to_all(parts, axes, split_axis=0, concat_axis=0, tiled=True)
    row = lax.broadcasted_iota(jnp.int32, (2 * owners * ROWS, LANES), 0)
    lane = lax.broadcasted_iota(jnp.int32, (2 * owners * ROWS, LANES), 1)
    freq = my_rank + owners * (row % ROWS)
    coarse = jnp.stack(phase_pair((row // ROWS) * freq, sample_total // LANES, -1.0))
    fine = jnp.stack(phase_pair(lane * (freq + owners * SFT_DEV * (row // ROWS)), sample_total, -1.0))
    fine = fine * (1.0 / math.sqrt(sample_total))
    operands = [parts, totals, coarse, fine, jnp.asarray(forward_table())]
    f_stat = pl.pallas_call(
        functools.partial(statistic_kernel, sample_total),
        out_shape=jax.ShapeDtypeStruct((tmpl_local, NQ, LANES), f32),
        in_specs=[vmem()] * len(operands),
        out_specs=vmem(),
        name="statistic",
    )(*[resident(operand) for operand in operands])
    return f_stat[:, :, None, :]


def solution(mesh):
    owners = mesh.shape["tm"] * mesh.shape["band"]
    one_run_each = NB // RUN == owners and mesh.shape["band"] == 2
    in_specs = (
        P(None, ("groups", "tm"), "band"),
        P(("groups", "tmpl"), None, ("tm", "band")),
        P(("groups", "tmpl"), None, None, ("tm", "band")),
    )
    out_specs = P(("groups", "tmpl"), None, ("tm", "band"), None)
    return jax.shard_map(
        run_device if one_run_each else per_device,
        mesh=mesh,
        in_specs=in_specs,
        out_specs=out_specs,
        check_vma=False,
    )
```

```python
import functools
import math

import jax
import jax.numpy as jnp
import numpy as np
from jax import lax
from jax.experimental import pallas as pl
from jax.experimental.pallas import tpu as pltpu
from jax.sharding import PartitionSpec as P

NB = 2048
NQ = 128
NP = 16
SFT_DEV = 8
MAXD = 1000
NFRAC = 8
RUN = 256


stat_eps = 1e-06
floor_share = 0.5


def shifted(value, axis, by):
    length = lax.axis_size(axis)
    pairs = [(i, i + by) for i in range(length) if 0 <= i + by < length]
    return lax.ppermute(value, axis, pairs)


def lagrange(fraction):
    return (
        -fraction * (fraction - 1.0) * (fraction - 2.0) / 6.0,
        (fraction + 1.0) * (fraction - 1.0) * (fraction - 2.0) / 2.0,
        -(fraction + 1.0) * fraction * (fraction - 2.0) / 2.0,
        (fraction + 1.0) * fraction * (fraction - 1.0) / 6.0,
    )


def phase_pair(product, modulus, direction):
    angles = direction * 2.0 * math.pi / modulus * (product % modulus).astype(jnp.float32)
    return (jnp.cos(angles), jnp.sin(angles))


def dft_table(length, direction):
    rows_at = lax.broadcasted_iota(jnp.int32, (length, length), 0)
    cols_at = lax.broadcasted_iota(jnp.int32, (length, length), 1)
    return phase_pair(rows_at * cols_at, length, direction)


def complex_einsum(pattern, lhs_pair, rhs_pair):
    lhs_real, lhs_imag = lhs_pair
    rhs_real, rhs_imag = rhs_pair
    high = lax.Precision.HIGHEST
    out_real = jnp.einsum(pattern, lhs_real, rhs_real, precision=high) - jnp.einsum(
        pattern, lhs_imag, rhs_imag, precision=high
    )
    out_imag = jnp.einsum(pattern, lhs_real, rhs_imag, precision=high) + jnp.einsum(
        pattern, lhs_imag, rhs_real, precision=high
    )
    return (out_real, out_imag)


def rotate(values, phases):
    val_real, val_imag = values
    cos_part, sin_part = phases
    return (val_real * cos_part - val_imag * sin_part, val_real * sin_part + val_imag * cos_part)


def apply_weights(arrived):
    return arrived[:, 1][:, :, None] * arrived[:, 0][:, None]


def finish(arrived):
    owners = lax.axis_size("tm") * lax.axis_size("band")
    my_rank = lax.axis_index("tm") * lax.axis_size("band") + lax.axis_index("band")
    q_local = arrived.shape[3]
    lane_width = arrived.shape[5]
    sample_total = SFT_DEV * owners * NB
    section_one = complex_einsum(
        "abqix,ic->abqcx", (arrived[:, :, 0], arrived[:, :, 1]), dft_table(owners, -1.0)
    )
    c_pos = lax.broadcasted_iota(jnp.int32, (owners, lane_width), 0)
    x_pos = lax.broadcasted_iota(jnp.int32, (owners, lane_width), 1)
    section_one = rotate(section_one, phase_pair(c_pos * (x_pos // NP), SFT_DEV * owners, -1.0))
    short_table = dft_table(SFT_DEV, -1.0)
    ident_rows = jnp.eye(NP, dtype=jnp.float32)
    spread = (jnp.kron(short_table[0], ident_rows), jnp.kron(short_table[1], ident_rows))
    section_two = complex_einsum("abqcx,xy->abqcy", section_one, spread)
    q_grid = my_rank * q_local + lax.broadcasted_iota(jnp.int32, (q_local, owners, lane_width), 0)
    c_grid = lax.broadcasted_iota(jnp.int32, (q_local, owners, lane_width), 1)
    x_grid = lax.broadcasted_iota(jnp.int32, (q_local, owners, lane_width), 2)
    time_index = x_grid % NP + NP * q_grid
    freq_index = c_grid + owners * (x_grid // NP)
    section_two = rotate(section_two, phase_pair(time_index * freq_index, sample_total, -1.0))
    packed = jnp.stack(section_two, axis=2)
    turned = lax.all_to_all(packed, ("tm", "band"), split_axis=4, concat_axis=3, tiled=True)
    turned = turned.reshape(turned.shape[0], 2, 2, NQ, lane_width)
    section_three = complex_einsum(
        "abqx,qv->abvx", (turned[:, :, 0], turned[:, :, 1]), dft_table(NQ, -1.0)
    )
    v_pos = lax.broadcasted_iota(jnp.int32, (NQ, lane_width), 0)
    p_pos = lax.broadcasted_iota(jnp.int32, (NQ, lane_width), 1) % NP
    section_three = rotate(section_three, phase_pair(v_pos * p_pos, NB, -1.0))
    fine_table = dft_table(NP, -1.0)
    ident_blocks = jnp.eye(SFT_DEV, dtype=jnp.float32)
    block_table = (jnp.kron(ident_blocks, fine_table[0]), jnp.kron(ident_blocks, fine_table[1]))
    result = complex_einsum("abvx,xy->abvy", section_three, block_table)
    return jnp.stack(result, axis=2)


def per_device(sft_bins, delay_code, antenna):
    owners = lax.axis_size("tm") * lax.axis_size("band")
    sample_total = SFT_DEV * owners * NB
    spectra = lax.all_to_all(sft_bins, "band", split_axis=1, concat_axis=2, tiled=True)
    bin_grid = spectra.reshape(2, SFT_DEV, NP, NQ)
    section_one = complex_einsum("pk,skl->spl", dft_table(NP, 1.0), (bin_grid[0], bin_grid[1]))
    p_rows = lax.broadcasted_iota(jnp.int32, (NP, NQ), 0)
    l_cols = lax.broadcasted_iota(jnp.int32, (NP, NQ), 1)
    section_one = rotate(section_one, phase_pair(p_rows * l_cols, NB, 1.0))
    series_pair = complex_einsum("spl,lq->spq", section_one, dft_table(NQ, 1.0))
    norm_scale = 1.0 / math.sqrt(NB)
    stacked = jnp.stack([series_pair[0] * norm_scale, series_pair[1] * norm_scale])
    rim_cols = (MAXD + 1 + NP) // NP
    head_rim = stacked[:, 0, :, :rim_cols]
    tail_rim = stacked[:, SFT_DEV - 1, :, NQ - rim_cols :]
    after_rim = shifted(head_rim, ("tm", "band"), -1)
    before = shifted(tail_rim, ("tm", "band"), 1)
    rim_size = NP * rim_cols
    span_len = SFT_DEV * NB
    timed = stacked.transpose(0, 1, 3, 2).reshape(2, span_len)
    before_timed = before.transpose(0, 2, 1).reshape(2, rim_size)
    after_timed = after_rim.transpose(0, 2, 1).reshape(2, rim_size)
    buffer = jnp.concatenate([before_timed, timed, after_timed], axis=1)
    lane_width = SFT_DEV * NP
    tmpl_local = delay_code.shape[0]
    run_count = span_len // RUN
    code_time = (
        delay_code.reshape(tmpl_local, NQ, SFT_DEV, NP)
        .transpose(0, 2, 1, 3)
        .reshape(tmpl_local, run_count, RUN)
    )
    offsets = code_time[:, :, 0] // NFRAC - MAXD
    run_starts = (jnp.arange(run_count, dtype=jnp.int32) * RUN)[None, :] + offsets + (rim_size - 1)

    def take_segment(start):
        return lax.dynamic_slice_in_dim(buffer, start, RUN + 3, 1)

    segments = jax.vmap(jax.vmap(take_segment))(run_starts)
    fraction = (code_time % NFRAC).astype(jnp.float32) / NFRAC
    coeffs = lagrange(fraction)
    res_time = coeffs[0][:, :, None, :] * segments[:, :, :, 0:RUN]
    for tap_index in range(1, 4):
        res_time = (
            res_time
            + coeffs[tap_index][:, :, None, :] * segments[:, :, :, tap_index : tap_index + RUN]
        )
    resampled = res_time.transpose(0, 2, 1, 3).reshape(tmpl_local, 2, SFT_DEV, NQ, NP)
    resampled = resampled.transpose(0, 1, 3, 2, 4).reshape(tmpl_local, 2, NQ, lane_width)
    weight_a = antenna[:, 0]
    weight_b = antenna[:, 1]
    local_sums = jnp.stack(
        [
            jnp.sum(weight_a * weight_a, axis=(1, 2)),
            jnp.sum(weight_b * weight_b, axis=(1, 2)),
            jnp.sum(weight_a * weight_b, axis=(1, 2)),
        ],
        axis=1,
    )
    totals = lax.psum(local_sums, ("tm", "band"))
    payload = jnp.stack([resampled, antenna], axis=1)
    spectra_out = finish(
        apply_weights(
            lax.all_to_all(
                payload[:, :, :, :, None, :],
                ("tm", "band"),
                split_axis=3,
                concat_axis=4,
                tiled=True,
            )
        )
    )
    out_scale = 1.0 / math.sqrt(sample_total)
    a_real = spectra_out[:, 0, 0] * out_scale
    a_imag = spectra_out[:, 0, 1] * out_scale
    b_real = spectra_out[:, 1, 0] * out_scale
    b_imag = spectra_out[:, 1, 1] * out_scale
    power_a = (totals[:, 0] / sample_total + stat_eps)[:, None, None]
    power_b = (totals[:, 1] / sample_total + stat_eps)[:, None, None]
    cross_ab = (totals[:, 2] / sample_total)[:, None, None]
    det_floor = jnp.maximum(
        power_a * power_b - cross_ab * cross_ab, floor_share * power_a * power_b
    )
    f_stat = (
        power_b * (a_real * a_real + a_imag * a_imag)
        + power_a * (b_real * b_real + b_imag * b_imag)
        - 2.0 * cross_ab * (a_real * b_real + a_imag * b_imag)
    ) / det_floor
    return f_stat[:, :, None, :]


LANES = 128
ROWS = 8
HALO = 2


def split_table(table):
    high = table.astype(jnp.bfloat16)
    low = (table - high.astype(np.float64)).astype(jnp.bfloat16)
    return np.stack([high, low])


def unit(product, modulus, sign):
    angle = sign * 2.0 * np.pi / modulus * (product % modulus)
    return np.cos(angle), np.sin(angle)


def inverse_tables():
    p_at = np.arange(NP)[:, None]
    l_at = np.arange(NQ)[None, :]
    twist = np.stack(unit(p_at * l_at, NB, 1.0)) / math.sqrt(NB)
    real, imag = unit(np.arange(NQ)[:, None] * l_at, NQ, 1.0)
    full = np.block([[real, -imag], [imag, real]])
    return twist.astype(np.float32), split_table(full)


def forward_table():
    lane = np.arange(LANES)
    bins = ROWS * (lane % NP) + lane // NP
    real, imag = unit(np.arange(LANES)[:, None] * bins[None, :], LANES, -1.0)
    return split_table(np.block([[real, imag], [-imag, real]]))


def add(one, two):
    return one[0] + two[0], one[1] + two[1]


def sub(one, two):
    return one[0] - two[0], one[1] - two[1]


def turn(value, step, length, sign):
    real, imag = value
    step = step % length
    if step == 0:
        return value
    if 2 * step == length:
        return -real, -imag
    if 4 * step == length:
        return (-imag, real) if sign > 0 else (imag, -real)
    if 4 * step == 3 * length:
        return (imag, -real) if sign > 0 else (-imag, real)
    angle = sign * 2.0 * math.pi * step / length
    cos_part, sin_part = math.cos(angle), math.sin(angle)
    if 8 * step == length:
        root = math.sqrt(0.5)
        if sign > 0:
            return (real - imag) * root, (real + imag) * root
        return (real + imag) * root, (imag - real) * root
    return real * cos_part - imag * sin_part, real * sin_part + imag * cos_part


def small_fft(values, sign):
    length = len(values)
    if length == 1:
        return values
    if length == 2:
        return [add(values[0], values[1]), sub(values[0], values[1])]
    even = small_fft(values[0::2], sign)
    odd = small_fft(values[1::2], sign)
    half = length // 2
    turned = [turn(odd[k], k, length, sign) for k in range(half)]
    return [add(even[k], turned[k]) for k in range(half)] + [sub(even[k], turned[k]) for k in range(half)]


def times(value, cos_part, sin_part):
    real, imag = value
    return real * cos_part - imag * sin_part, real * sin_part + imag * cos_part


def block_transposes(tiles):
    row = lax.broadcasted_iota(jnp.int32, (ROWS, LANES), 0)
    group = lax.broadcasted_iota(jnp.int32, (ROWS, LANES), 1) // NP
    gather_at = (group + row) & (ROWS - 1)
    reverse_at = (ROWS - row) & (ROWS - 1)
    tiles = [pltpu.roll(tile, 0, 1, stride=NP, stride_axis=0) for tile in tiles]
    tiles = [jnp.take_along_axis(tile, gather_at, axis=0) for tile in tiles]
    tiles = [pltpu.roll(tile, 0, 1, stride=NP, stride_axis=0) for tile in tiles]
    return [jnp.take_along_axis(tile, reverse_at, axis=0) for tile in tiles]


def split_dot(lhs, rhs, dims):
    out = None
    for one, two in ((0, 0), (0, 1), (1, 0)):
        part = lax.dot_general(lhs[one], rhs[two], dims, preferred_element_type=jnp.float32)
        out = part if out is None else out + part
    return out


def split_value(value):
    high = value.astype(jnp.bfloat16)
    return high, (value - high.astype(jnp.float32)).astype(jnp.bfloat16)


def prepare_kernel(code_ref, antenna_ref, bins_ref, fraction_ref, weights_ref, sums_ref, start_ref, shift_ref, mine_ref):
    mine_ref[...] = bins_ref[...]
    tmpl_local = code_ref.shape[0]
    owners = code_ref.shape[1] // (2 * ROWS)
    lane = lax.broadcasted_iota(jnp.int32, (ROWS, LANES), 1)
    row = lax.broadcasted_iota(jnp.int32, (ROWS, LANES), 0)
    for t in range(tmpl_local):
        for h in range(2):
            codes = [code_ref[t, pl.ds(2 * ROWS * j + ROWS * h, ROWS), :] for j in range(owners)]
            turned = block_transposes(codes)
            if h == 0:
                starts = jnp.zeros((ROWS, LANES), jnp.int32)
                for j in range(owners):
                    whole = jnp.broadcast_to(turned[j][:, 0:1], (ROWS, LANES)) // NFRAC - MAXD
                    start = whole + (row * owners + j) * RUN + (NB - 1)
                    starts = jnp.where(lane == j, start, starts)
                    shift_ref[pl.ds(t * SFT_DEV * owners + j, ROWS, stride=owners), :] = start & (LANES - 1)
                start_ref[pl.ds(t * ROWS, ROWS), :] = starts
            for j in range(owners):
                level = (turned[j] & (NFRAC - 1)).astype(jnp.float32) * (1.0 / NFRAC)
                fraction_ref[pl.ds((t * SFT_DEV * 2 + h) * ROWS + j, ROWS, stride=2 * ROWS), :] = level
        sums = [jnp.zeros((ROWS, LANES), jnp.float32) for _ in range(3)]
        for h in range(2):
            places = [pl.ds(2 * ROWS * j + ROWS * h, ROWS) for j in range(owners)]
            one = [antenna_ref[t, 0, place, :] for place in places]
            two = [antenna_ref[t, 1, place, :] for place in places]
            for first, second in zip(one, two):
                sums = [sums[0] + first * first, sums[1] + second * second, sums[2] + first * second]
            for w, tiles in ((0, one), (1, two)):
                turned = block_transposes(tiles)
                for j in range(owners):
                    at = ((t * 2 + w) * SFT_DEV * 2 + h) * ROWS + j
                    weights_ref[pl.ds(at, ROWS, stride=2 * ROWS), :] = turned[j]
        for index in range(3):
            sums_ref[pl.ds(t * 4 + index, 1), :] = jnp.sum(sums[index], axis=0, keepdims=True)
        sums_ref[pl.ds(t * 4 + 3, 1), :] = jnp.zeros((1, LANES), jnp.float32)


def pack_kernel(band_ref, mine_ref, far_ref, out_ref):
    first = band_ref[0] == 0
    half = NP // 2
    last = mine_ref.shape[1] - 1
    for part in range(2):
        for kappa in range(half):
            cols = pl.ds(LANES * kappa, LANES)
            mine, far = [
                jnp.where(first, ref[part, pl.ds(last, 1), cols], ref[part, pl.ds(0, 1), cols])
                for ref in (mine_ref, far_ref)
            ]
            out_ref[part, pl.ds(kappa, 1), :] = jnp.where(first, mine, far)
            out_ref[part, pl.ds(kappa + half, 1), :] = jnp.where(first, far, mine)


def inverse_columns(values, twist_ref, z_ref, places):
    values = small_fft(values, 1.0)
    for p in range(NP):
        turned = times(values[p], twist_ref[0, pl.ds(p, 1), :], twist_ref[1, pl.ds(p, 1), :])
        for part in range(2):
            z_ref[part, places[p], :] = turned[part]


def inverse_grid(table_ref, z_ref):
    z_value = split_value(jnp.concatenate([z_ref[0], z_ref[1]], axis=1))
    return split_dot((table_ref[0], table_ref[1]), z_value, (((1,), (1,)), ((), ())))


def halo_rows(grid, part, late):
    per_sft = NB // LANES
    tiles = [grid[NQ * part + ROWS * r : NQ * part + ROWS * (r + 1)] for r in range(per_sft)]
    tiles = [jnp.where(late, tiles[r + per_sft // 2], tiles[r]) for r in range(per_sft // 2)]
    return [tile[0:1] for tile in block_transposes(tiles)]


def late_row():
    return NB // LANES


def early_row():
    return 2 * (NB // LANES) * (SFT_DEV + 1)


def align_runs(time_ref, start_ref, run_ref, s_local, place):
    tmpl_local = start_ref.shape[0] // SFT_DEV
    owners = NB // RUN
    starts = [start_ref[t * SFT_DEV + s_local, j] for t in range(tmpl_local) for j in range(owners)]
    tiles = [time_ref[pl.ds((start >> 7) * 2, ROWS), :] for start in starts]
    tiles = [pltpu.roll(tile, (-start) & (LANES - 1), 1) for tile, start in zip(tiles, starts)]
    for at, tile in enumerate(tiles):
        run_ref[pl.ds((place * len(tiles) + at) * ROWS, ROWS), :] = tile


def combine_runs(run_ref, shift_ref, fraction_ref, weights_ref, flat_ref, slot, s_local, place):
    tmpl_local = shift_ref.shape[0] // (SFT_DEV * ROWS)
    owners = NB // RUN
    lane = lax.broadcasted_iota(jnp.int32, (ROWS, LANES), 1)

    def rows_at(group):
        return pl.ds(group * ROWS if isinstance(group, int) else pl.multiple_of(group * ROWS, ROWS), ROWS)

    for t in range(tmpl_local):
        straight = lane < LANES - shift_ref[rows_at(t * SFT_DEV + s_local), :]
        rows = []
        for part in range(2):
            base = (place * tmpl_local + t) * owners * ROWS + part
            raw = [run_ref[pl.ds(base + 2 * i, ROWS, stride=ROWS), :] for i in range(4)]
            rows.append([jnp.where(straight, raw[i], raw[i + 1]) for i in range(3)])
        at = (t * SFT_DEV + s_local) * 2
        coeffs = [lagrange(fraction_ref[rows_at(at + h), :]) for h in range(2)]
        totals = [[coeffs[h][0] * rows[part][h] for h in range(2)] for part in range(2)]
        for k in range(1, 4):
            rolled = [[pltpu.roll(tile, LANES - k, 1) for tile in rows[part]] for part in range(2)]
            for part in range(2):
                for h in range(2):
                    tap = jnp.where(lane < LANES - k, rolled[part][h], rolled[part][h + 1])
                    totals[part][h] = totals[part][h] + coeffs[h][k] * tap
        for w in range(2):
            at = ((t * 2 + w) * SFT_DEV + s_local) * 2
            for h in range(2):
                weight = weights_ref[rows_at(at + h), :]
                for part in range(2):
                    to = (part * SFT_DEV + s_local) * ROWS + t * 4 + w * 2 + h
                    flat_ref[pl.ds(to, owners, stride=slot), :] = totals[part][h] * weight


def series_kernel(
    band_ref,
    mine_ref,
    far_ref,
    twist_ref,
    table_ref,
    start_in_ref,
    shift_ref,
    fraction_ref,
    weights_ref,
    sums_ref,
    time_ref,
    out_ref,
    z_ref,
    run_ref,
    start_ref,
    copy_sem,
):
    starts_copy = pltpu.make_async_copy(start_in_ref, start_ref, copy_sem)
    starts_copy.start()
    owners, slot = out_ref.shape[:2]
    band = band_ref[0]
    first = band == 0
    half = NP // 2
    per_sft = NB // LANES
    own = [[None, None] for _ in range(NP)]
    inner = [[None, None] for _ in range(NP)]
    for part in range(2):
        for kappa in range(half):
            cols = pl.ds(LANES * kappa, LANES)
            rows = pl.ds(pl.multiple_of(band * SFT_DEV, SFT_DEV), SFT_DEV)
            mine, far = mine_ref[part, rows, cols], far_ref[part, rows, cols]
            own[kappa][part] = jnp.where(first, mine, far)
            own[kappa + half][part] = jnp.where(first, far, mine)
            mine, far = [
                jnp.where(first, ref[part, pl.ds(SFT_DEV, 1), cols], ref[part, pl.ds(SFT_DEV - 1, 1), cols])
                for ref in (mine_ref, far_ref)
            ]
            inner[kappa][part] = jnp.where(first, mine, far)
            inner[kappa + half][part] = jnp.where(first, far, mine)
    inverse_columns([tuple(v) for v in own], twist_ref, z_ref, [pl.ds(p, ROWS, stride=NP) for p in range(NP)])
    inverse_columns([tuple(v) for v in inner], twist_ref, z_ref, [pl.ds(LANES + p, 1) for p in range(NP)])
    z_ref[:, pl.ds(LANES + NP, LANES - NP), :] = jnp.zeros((2, LANES - NP, LANES), jnp.float32)
    grid = inverse_grid(table_ref, z_ref)
    inner_row = jnp.where(first, early_row(), late_row())
    for part in range(2):
        tiles = [grid[NQ * part + ROWS * r : NQ * part + ROWS * (r + 1), :LANES] for r in range(per_sft)]
        tiles = block_transposes(tiles)
        for r in range(per_sft):
            time_ref[pl.ds(2 * (per_sft + r) + part, ROWS, stride=2 * per_sft), :] = tiles[r]
        tiles = halo_rows(grid[:, LANES:], part, jnp.logical_not(first))
        for r in range(per_sft // 2):
            time_ref[pl.ds(inner_row + 2 * r + part, 1), :] = tiles[r]


    for j in range(owners):
        out_ref[j, pl.ds(slot - ROWS, ROWS), :] = sums_ref[...]
    starts_copy.wait()
    flat_ref = out_ref.reshape(owners * slot, LANES)
    order = list(range(1, SFT_DEV - 1)) + [jnp.where(first, SFT_DEV - 1, 0)]
    for place, s_local in enumerate(order):
        align_runs(time_ref, start_ref, run_ref, s_local, place)
    for place, s_local in enumerate(order):
        combine_runs(run_ref, shift_ref, fraction_ref, weights_ref, flat_ref, slot, s_local, place)


def resample_kernel(
    band_ref,
    start_in_ref,
    series_ref,
    outer_ref,
    shift_ref,
    fraction_ref,
    weights_ref,
    twist_ref,
    table_ref,
    partial_ref,
    out_ref,
    z_ref,
    time_ref,
    run_ref,
    start_ref,
    copy_sem,
):
    starts_copy = pltpu.make_async_copy(start_in_ref, start_ref, copy_sem)
    starts_copy.start()
    first = band_ref[0] == 0
    owners, slot = out_ref.shape[:2]
    values = [tuple(outer_ref[part, pl.ds(kappa, 1), :] for part in range(2)) for kappa in range(NP)]
    z_ref[:, pl.ds(NP, LANES - NP), :] = jnp.zeros((2, LANES - NP, LANES), jnp.float32)
    inverse_columns(values, twist_ref, z_ref, [pl.ds(p, 1) for p in range(NP)])
    grid = inverse_grid(table_ref, z_ref)
    time_ref[...] = series_ref[...]
    outer_row = jnp.where(first, late_row(), early_row())
    for part in range(2):
        tiles = halo_rows(grid, part, first)
        for r in range(NB // LANES // 2):
            time_ref[pl.ds(outer_row + 2 * r + part, 1), :] = tiles[r]
    starts_copy.wait()
    flat_ref = out_ref.reshape(owners * slot, LANES)
    s_local = jnp.where(first, 0, SFT_DEV - 1)
    align_runs(time_ref, start_ref, run_ref, s_local, 0)
    combine_runs(run_ref, shift_ref, fraction_ref, weights_ref, flat_ref, slot, s_local, 0)


def section_kernel(samples_ref, out_ref, sums_ref, mid_ref):
    owners = samples_ref.shape[0]
    slot = samples_ref.shape[1]
    for s_local in range(SFT_DEV):
        values = [
            tuple(samples_ref[i, pl.ds((part * SFT_DEV + s_local) * ROWS, ROWS), :] for part in range(2))
            for i in range(owners)
        ]
        values = small_fft(values, -1.0)
        for c in range(owners):
            turned = turn(values[c], c * s_local, owners * SFT_DEV, -1.0)
            for part in range(2):
                mid_ref[part, pl.ds((c * SFT_DEV + s_local) * ROWS, ROWS), :] = turned[part]
    for c in range(owners):
        values = []
        for s_local in range(SFT_DEV):
            rows = pl.ds((c * SFT_DEV + s_local) * ROWS, ROWS)
            values.append((mid_ref[0, rows, :], mid_ref[1, rows, :]))
        values = small_fft(values, -1.0)
        for d in range(SFT_DEV):
            for part in range(2):
                out_ref[c, pl.ds(part * ROWS * ROWS + d, ROWS, stride=ROWS), :] = values[d][part]
    total = samples_ref[0, pl.ds(slot - ROWS, ROWS), :]
    for i in range(1, owners):
        total = total + samples_ref[i, pl.ds(slot - ROWS, ROWS), :]
    sums_ref[...] = jnp.broadcast_to(jnp.sum(total, axis=1, keepdims=True), (ROWS, LANES))


def statistic_kernel(sample_total, parts_ref, sums_ref, coarse_ref, fine_ref, table_ref, out_ref):
    rhs = (table_ref[0], table_ref[1])
    dims = (((1,), (0,)), ((), ()))
    tmpl_local = out_ref.shape[0]
    owners = parts_ref.shape[0]
    for t in range(tmpl_local):
        spectra = []
        for w in range(2):
            values = []
            for rho in range(2 * owners):
                j, h = rho // 2, rho % 2
                base = (t * 4 + w * 2 + h) * ROWS
                value = tuple(parts_ref[j, pl.ds(part * ROWS * ROWS + base, ROWS), :] for part in range(2))
                rows = pl.ds(rho * ROWS, ROWS)
                values.append(times(value, coarse_ref[0, rows, :], coarse_ref[1, rows, :]))
            values = small_fft(values, -1.0)
            values = [
                times(values[a], fine_ref[0, pl.ds(a * ROWS, ROWS), :], fine_ref[1, pl.ds(a * ROWS, ROWS), :])
                for a in range(2 * owners)
            ]
            real = jnp.concatenate([value[0] for value in values], axis=0)
            imag = jnp.concatenate([value[1] for value in values], axis=0)
            lhs = split_value(jnp.concatenate([real, imag], axis=1))
            out = split_dot(lhs, rhs, dims)
            spectra.append((out[:, :LANES], out[:, LANES:]))
        (a_real, a_imag), (b_real, b_imag) = spectra
        power_a = sums_ref[pl.ds(t * 4, 1), :] * (1.0 / sample_total) + stat_eps
        power_b = sums_ref[pl.ds(t * 4 + 1, 1), :] * (1.0 / sample_total) + stat_eps
        cross_ab = sums_ref[pl.ds(t * 4 + 2, 1), :] * (1.0 / sample_total)
        det_floor = jnp.maximum(power_a * power_b - cross_ab * cross_ab, floor_share * power_a * power_b)
        f_stat = (
            (power_b / det_floor) * (a_real * a_real + a_imag * a_imag)
            + (power_a / det_floor) * (b_real * b_real + b_imag * b_imag)
            - (2.0 * cross_ab / det_floor) * (a_real * b_real + a_imag * b_imag)
        )
        tiles = block_transposes([f_stat[a * ROWS : (a + 1) * ROWS] for a in range(2 * owners)])
        for a in range(2 * owners):
            out_ref[t, pl.ds(a, ROWS, stride=2 * owners), :] = tiles[a]


def vmem():
    return pl.BlockSpec(memory_space=pltpu.VMEM)


def resident(value):
    return pltpu.with_memory_space_constraint(value, pltpu.VMEM)


def run_device(sft_bins, delay_code, antenna):
    axes = ("tm", "band")
    owners = lax.axis_size("tm") * lax.axis_size("band")
    my_rank = lax.axis_index("tm") * lax.axis_size("band") + lax.axis_index("band")
    sample_total = SFT_DEV * owners * NB
    tmpl_local = delay_code.shape[0]
    f32 = jnp.float32
    slot = SFT_DEV * ROWS
    time_rows = 2 * (SFT_DEV + 2) * NB // LANES
    smem = pl.BlockSpec(memory_space=pltpu.SMEM)
    band = lax.axis_index("band").astype(jnp.int32).reshape(1)
    far = lax.ppermute(sft_bins, "band", [(0, 1), (1, 0)])
    fraction, weights, sums, starts, shifts, mine = pl.pallas_call(
        prepare_kernel,
        out_shape=(
            pltpu.VMEM((tmpl_local * SFT_DEV * 2 * ROWS, LANES), f32),
            pltpu.VMEM((tmpl_local * 2 * SFT_DEV * 2 * ROWS, LANES), f32),
            pltpu.VMEM((ROWS, LANES), f32),
            pltpu.VMEM((tmpl_local * SFT_DEV, LANES), jnp.int32),
            pltpu.VMEM((tmpl_local * SFT_DEV * owners, LANES), jnp.int32),
            pltpu.VMEM(sft_bins.shape, f32),
        ),
        in_specs=[vmem()] * 3,
        out_specs=(vmem(),) * 6,
        name="prepare",
    )(delay_code, antenna, sft_bins)
    row = lax.broadcasted_iota(jnp.int32, (2 * owners * ROWS, LANES), 0)
    lane = lax.broadcasted_iota(jnp.int32, (2 * owners * ROWS, LANES), 1)
    freq = my_rank + owners * (row % ROWS)
    coarse = jnp.stack(phase_pair((row // ROWS) * freq, sample_total // LANES, -1.0))
    fine = jnp.stack(phase_pair(lane * (freq + owners * SFT_DEV * (row // ROWS)), sample_total, -1.0))
    fine = fine * (1.0 / math.sqrt(sample_total))
    last_table = jnp.asarray(forward_table())
    coarse, fine, last_table = resident(coarse), resident(fine), resident(last_table)
    far, mine = resident(far), resident(mine)
    mine, coarse, fine, last_table = lax.optimization_barrier((mine, coarse, fine, last_table))
    mine = resident(mine)
    edge = pl.pallas_call(
        pack_kernel,
        out_shape=pltpu.VMEM((2, NP, LANES), f32),
        in_specs=[smem, vmem(), vmem()],
        out_specs=vmem(),
        name="pack",
    )(band, mine, far)
    along = [(rank, rank + 2) for rank in range(0, owners - 2, 2)]
    along += [(rank, rank - 2) for rank in range(3, owners, 2)]
    outer = lax.ppermute(edge, axes, along)
    twist, inverse_table = [resident(jnp.asarray(table)) for table in inverse_tables()]
    fraction, weights, sums, starts, shifts = [
        resident(value) for value in (fraction, weights, sums, starts, shifts)
    ]
    payload = pltpu.VMEM((owners, 2 * slot + ROWS, LANES), f32)
    scratch = [
        pltpu.SMEM((tmpl_local * SFT_DEV, LANES), jnp.int32),
        pltpu.SemaphoreType.DMA,
    ]
    series, partial = pl.pallas_call(
        series_kernel,
        out_shape=(pltpu.VMEM((time_rows, LANES), f32), payload),
        in_specs=[smem] + [vmem()] * 9,
        out_specs=(vmem(), vmem()),
        scratch_shapes=[
            pltpu.VMEM((2, 2 * LANES, LANES), f32),
            pltpu.VMEM(((SFT_DEV - 1) * tmpl_local * owners * ROWS, LANES), f32),
        ]
        + scratch,
        name="series",
    )(band, mine, far, twist, inverse_table, starts, shifts, fraction, weights, sums)
    operands = [starts, resident(series), resident(outer), shifts, fraction, weights, twist, inverse_table]
    operands += [resident(partial)]
    samples = pl.pallas_call(
        resample_kernel,
        out_shape=payload,
        in_specs=[smem] + [vmem()] * len(operands),
        out_specs=vmem(),
        scratch_shapes=[
            pltpu.VMEM((2, LANES, LANES), f32),
            pltpu.VMEM((time_rows, LANES), f32),
            pltpu.VMEM((tmpl_local * owners * ROWS, LANES), f32),
        ]
        + scratch,
        input_output_aliases={len(operands): 0},
        name="resample",
    )(band, *operands)
    samples = lax.all_to_all(samples, axes, split_axis=0, concat_axis=0, tiled=True)
    parts, totals = pl.pallas_call(
        section_kernel,
        out_shape=(pltpu.VMEM((owners, 2 * slot, LANES), f32), pltpu.VMEM((ROWS, LANES), f32)),
        in_specs=[vmem()],
        out_specs=(vmem(), vmem()),
        scratch_shapes=[pltpu.VMEM((2, owners * slot, LANES), f32)],
        name="section",
    )(resident(samples))
    parts = lax.all_to_all(resident(parts), axes, split_axis=0, concat_axis=0, tiled=True)
    operands = [parts, totals, coarse, fine, last_table]
    f_stat = pl.pallas_call(
        functools.partial(statistic_kernel, sample_total),
        out_shape=jax.ShapeDtypeStruct((tmpl_local, NQ, LANES), f32),
        in_specs=[vmem()] * len(operands),
        out_specs=vmem(),
        name="statistic",
    )(*[resident(operand) for operand in operands])
    return f_stat[:, :, None, :]


def solution(mesh):
    owners = mesh.shape["tm"] * mesh.shape["band"]
    one_run_each = NB // RUN == owners and mesh.shape["band"] == 2
    in_specs = (
        P(None, ("groups", "tm"), "band"),
        P(("groups", "tmpl"), None, ("tm", "band")),
        P(("groups", "tmpl"), None, None, ("tm", "band")),
    )
    out_specs = P(("groups", "tmpl"), None, ("tm", "band"), None)
    return jax.shard_map(
        run_device if one_run_each else per_device,
        mesh=mesh,
        in_specs=in_specs,
        out_specs=out_specs,
        check_vma=False,
    )
```
